32 devices in a mesh: groups: 2 (over y), seq: 4 (over z), lang: 2 (over x), panel: 2 (over core).
Axes of the slice: x: 2, y: 2, z: 4, core: 2. Of those that a mesh axis runs over, the one named last changes fastest.
Arguments:
- text_rows: bfloat16 [128, 1024], P(('groups', 'seq', 'lang', 'panel')), parts along dimension 0, may hold values from -40 to 40
- lang_ids: int32 [128, 1], P(('groups', 'seq', 'lang', 'panel')), parts along dimension 0, may hold values from 0 to 3; in each aligned block of 16 rows (0 to 15, 16 to 31, ...) at most 8 rows name the same one
- lang_map: int32 [4], replicated, may hold values from 0 to 3, each once
- durations: int32 [32, 4], P(('groups', 'seq', 'lang', 'panel')), parts along dimension 0, may hold values from 1 to 8, 24 in all within a row
- pos_table: float32 [8, 1024], replicated, may hold values from -6 to 6
- ln_gain: float32 [1024], replicated, may hold values from 0.25 to 1.75
- conv_weight: bfloat16 [4, 1024, 9, 4096], P(('lang', 'panel'), None, None, 'seq'), may hold values from -0.0625 to 0.0625
- conv_bias: float32 [4, 4096], P(('lang', 'panel'), 'seq'), may hold values from -3 to 3
- down_weight: bfloat16 [4, 4096, 1024], P(('lang', 'panel'), 'seq'), may hold values from -0.09375 to 0.09375
Outputs:
- unit_frames: bfloat16 [768, 1024], P(('groups', 'seq', 'lang', 'panel')), parts along dimension 0
The draws below stay inside these ranges and needn't reach their ends.
There are 2 independent parts, one for each index of `groups`. The reference program is written for one: setup_inputs(seed, part) draws one part's arguments, and reference() takes and returns one part's arrays. A program takes and returns all parts, laid end to end along the dimension named above; an argument that names none is the same for every part. Nothing has to cross between parts.
Inputs may be any that keep to these rules, and one draw needn't show every extreme that they name: `lang_ids`: rows are laid out shard after shard; in each aligned block of 16 rows (the text rows of the devices that share one index of seq) no language is named by more than 8 rows, and that many is reached in some block of every draw. `lang_map`: each language has its own expert slot. `durations`: each line sums to 24 frames, and some row of every line lasts 8 frames.
All inputs are finite; a program needn't handle non-finite values.
Results may differ from the reference program's by a relative error of at most 0.006.
Values may be sent and summed in bfloat16 or wider, within the bound.
A program may use at most 128 MiB of HBM per device.

```python
import math
import jax
import jax.numpy as jnp
import numpy as np
from jax import lax

D = 1024
FF = 4096
KW = 9
DMAX = 8
R_DEV = 4
MAXR = 8
FR_DEV = 24
EXPERTS = 4
SHARDS = 16
TEXT = 64
FRAMES = 384
N_SEQ = 4


def draw_text_rows(key, part):
    base_key, column_key, row_key = jax.random.split(key, 3)
    column_scale = jnp.exp(jax.random.uniform(column_key, (D,), jnp.float32, -1.2, 1.2))
    row_scale = jnp.exp(jax.random.uniform(row_key, (TEXT, 1), jnp.float32, -1.2, 1.2))
    values = jax.random.truncated_normal(base_key, -4.0, 4.0, (TEXT, D), jnp.float32)
    return (0.5 * values * column_scale[None, :] * row_scale).astype(jnp.bfloat16)


def level_of(rng, extent, cuts, least, largest):
    def one(dim, blocks):
        draws = jax.random.uniform(jax.random.fold_in(jax.random.fold_in(rng, 6), dim), (blocks,), jnp.float32, least / len(cuts), largest / len(cuts))
        return jnp.repeat(jnp.exp(draws), extent[dim] // blocks).reshape((-1,) + (1,) * (len(extent) - dim - 1))

    gain = one(*cuts[0])
    for cut in cuts[1:]:
        gain = gain * one(*cut)
    return gain


def split_up(count, total, limit, skew):
    weights = [(1 << 20) // math.isqrt(grade ** skew) + 1 for grade in range(2, count + 1)]
    surplus, given = total - limit - (count - 1), [1] * (count - 1)
    while surplus > 0:
        movable = [i for i in range(count - 1) if given[i] < limit]
        mass, left = sum([weights[i] for i in movable]), surplus
        for i in movable:
            extra = min(limit - given[i], max(1, left * weights[i] // mass), surplus)
            given[i] = given[i] + extra
            surplus = surplus - extra
    return np.array([limit] + given)


def uneven(own_key, amount, total, most, slope):
    if amount == 2:
        one = jax.random.randint(own_key, (), max(1, total - most), min(most, total - 1) + 1)
        return jnp.stack([one, total - one])
    tallies = jnp.asarray(split_up(amount, total, most, slope), jnp.int32)
    pairs = (amount - 1) // 2
    donor, sink = tallies[1:1 + 2 * pairs:2], tallies[2:2 + 2 * pairs:2]
    slack = jnp.minimum(donor - 1, most - sink)
    shifted = jax.random.randint(jax.random.fold_in(own_key, 1), (pairs,), 0, 1 << 20) % (slack + 1)
    tallies = tallies.at[1:1 + 2 * pairs:2].set(donor - shifted).at[2:2 + 2 * pairs:2].set(sink + shifted)
    return tallies[jax.random.permutation(jax.random.fold_in(own_key, 2), amount)]


def deal_out(key, own, number, rows, number_of, top, bound, skew):
    ranking = jax.random.permutation(key, number_of)
    packed, ordinary = portions_of(number_of, rows * top, bound, skew, True), portions_of(number_of, rows * top, bound, skew, False)
    places = jnp.arange(number_of)

    def named(tallies, turn):
        used = int((tallies > 0).sum())
        fixed = max(1, used // 4)
        passed = fixed + (places - fixed + turn * (used - fixed)) % max(1, number_of - fixed)
        return jnp.zeros((number_of,), jnp.int32).at[ranking[jnp.where(places < fixed, places, passed)]].set(jnp.asarray(tallies, jnp.int32))

    tallies = jnp.where(number % 4 == 0, named(packed, number // 4), named(ordinary, number - number // 4 - 1))
    mixed = jax.random.permutation(jax.random.fold_in(own, 3), number_of)
    giver, sink = mixed[0:number_of // 2 * 2:2], mixed[1:number_of // 2 * 2:2]
    room = jnp.minimum(tallies[giver] - 1, bound - tallies[sink]) // 2
    room = jnp.where((giver == ranking[0]) | (sink == ranking[0]) | (tallies[sink] == 0), 0, jnp.maximum(room, 0))
    passed = jax.random.randint(jax.random.fold_in(own, 4), (number_of // 2,), 0, 1 << 20) % (room + 1)
    tallies = tallies.at[giver].add(-passed).at[sink].add(passed)
    items = jnp.searchsorted(jnp.cumsum(tallies), jnp.arange(rows * top), side="right").astype(jnp.int32)
    table = items.reshape(top, rows).T
    table = table[jax.random.permutation(jax.random.fold_in(own, 1), rows)]
    turn = jax.random.randint(jax.random.fold_in(own, 2), (rows, 1), 0, top)
    return jnp.take_along_axis(table, (jnp.arange(top)[None, :] + turn) % top, axis=1)


def portions_of(count, total, most, lean, full):
    portions = [(1 << 20) // math.isqrt(grade ** lean) + 1 for grade in range(1, count + 1)]
    largest = most if full else min(most, max(-(-total // count), total * portions[0] // sum(portions)))
    least = 1 if total - largest >= count - 1 else 0
    given, spare = [largest] + [least] * (count - 1), total - largest - least * (count - 1)
    while spare > 0:
        free = [i for i in range(1, count) if given[i] < largest] or [i for i in range(1, count) if given[i] < most]
        pool, left = sum([portions[i] for i in free]), spare
        for i in free:
            addition = min(most - given[i], max(1, left * portions[i] // pool), spare)
            given[i] = given[i] + addition
            spare = spare - addition
    return np.array(given)


def gaussian(own_key, shape, scale, most, shards=(), kind=jnp.bfloat16):
    array = scale * jax.random.normal(own_key, shape, jnp.float32)
    if shards:
        array = array * level_of(own_key, shape, shards, -0.22, 0.18)
    return jnp.clip(array, -most, most).astype(kind)


def setup_inputs(seed: int = 0, part: int = 0) -> dict:
    arg_keys = jax.random.split(jax.random.key(seed), 10)
    part_splits = jax.random.split(jax.random.fold_in(arg_keys[9], part), 10)
    text_rows = draw_text_rows(jax.random.fold_in(jax.random.fold_in(arg_keys[9], part), 71), part)
    lang_ids_keys = jax.random.split(jax.random.fold_in(part_splits[1], 1), TEXT // (EXPERTS * R_DEV))
    lang_ids_turns = jax.random.permutation(jax.random.fold_in(part_splits[1], 3), TEXT // (EXPERTS * R_DEV))
    lang_ids = jax.vmap(lambda own, number: deal_out(jax.random.fold_in(part_splits[1], 2), own, number, EXPERTS * R_DEV, EXPERTS, 1, MAXR, 2))(lang_ids_keys, lang_ids_turns).reshape((TEXT, 1))
    lang_map = jax.random.permutation(arg_keys[2], EXPERTS).astype(jnp.int32)
    durations = jax.vmap(lambda own: uneven(own, R_DEV, FR_DEV, DMAX, 1))(jax.random.split(part_splits[3], SHARDS)).reshape((SHARDS, R_DEV)).astype(jnp.int32)
    pos_table = gaussian(arg_keys[4], (DMAX, D), 1.0, 6.0, (), jnp.float32)
    ln_gain = jnp.clip(1.0 + 0.15 * jax.random.normal(arg_keys[5], (D,), jnp.float32), 0.25, 1.75)
    conv_weight = gaussian(arg_keys[6], (EXPERTS, D, KW, FF), (KW * D) ** -0.5, 0.0625, ((0, 4), (3, 4)))
    conv_bias = gaussian(arg_keys[7], (EXPERTS, FF), 0.5, 3.0, ((0, 4), (1, 4)), jnp.float32)
    down_weight = gaussian(arg_keys[8], (EXPERTS, FF, D), FF ** -0.5, 0.09375, ((0, 4), (1, 4)))
    return {"text_rows": text_rows, "lang_ids": lang_ids, "lang_map": lang_map, "durations": durations, "pos_table": pos_table, "ln_gain": ln_gain, "conv_weight": conv_weight, "conv_bias": conv_bias, "down_weight": down_weight}


def layer_norm(values, ln_gain):
    center = values - lax.optimization_barrier(jnp.mean(values, axis=-1, keepdims=True))
    spread = lax.optimization_barrier(jnp.mean(center * center, axis=-1, keepdims=True))
    return center * lax.rsqrt(spread + 1e-05) * ln_gain

def expand_rows(row_values, lengths, pos_table, ln_gain):
    inputs = row_values[:, None, :] + pos_table[None, :, :]
    live_slot = jnp.arange(pos_table.shape[0], dtype=jnp.int32)[None, :] < lengths[:, None]
    normed = jnp.where(live_slot[:, :, None], layer_norm(inputs, ln_gain), jnp.zeros_like(inputs))
    return (inputs, normed.astype(jnp.bfloat16))

def shifted_sum(product, taps, slots):
    reach = taps // 2
    padded = jnp.pad(product, ((0, 0), (reach, reach), (0, 0), (0, 0)))
    total = padded[:, 0:slots, 0]
    for offset in range(1, taps):
        total = total + padded[:, offset:offset + slots, offset]
    return total

def reference(text_rows, lang_ids, lang_map, durations, pos_table, ln_gain, conv_weight, conv_bias, down_weight):
    expert_of = jnp.take(lang_map, lang_ids[:, 0], axis=0).astype(jnp.int32)
    lengths = durations.reshape(TEXT).astype(jnp.int32)
    holding = N_SEQ * MAXR
    order = jnp.arange(TEXT, dtype=jnp.int32)
    slice_width = FF // N_SEQ

    def one_expert(expert_slot):
        sort_key = jnp.where(expert_of == expert_slot, 0, TEXT).astype(jnp.int32) + order
        chosen = jnp.argsort(sort_key)[:holding].astype(jnp.int32)
        member = jnp.take(expert_of, chosen) == expert_slot
        chosen_len = jnp.where(member, jnp.take(lengths, chosen), 0).astype(jnp.int32)
        picked_rows = jnp.take(text_rows, chosen, axis=0).astype(jnp.float32)
        inputs, normed = expand_rows(picked_rows, chosen_len, pos_table, ln_gain)
        kernel = lax.dynamic_index_in_dim(conv_weight, expert_slot, 0, keepdims=False).astype(jnp.float32)
        kernel = kernel.reshape(D, KW * FF)
        flat = normed.reshape(holding * DMAX, D).astype(jnp.float32)
        product = jnp.dot(flat, kernel, precision=lax.Precision.HIGHEST).reshape(holding, DMAX, KW, FF)
        bias = lax.dynamic_index_in_dim(conv_bias, expert_slot, 0, keepdims=False)
        summed = shifted_sum(product, KW, DMAX) + bias[None, None, :]
        hidden = jax.nn.gelu(summed, approximate=False).astype(jnp.bfloat16).reshape(holding * DMAX, FF)
        down = lax.dynamic_index_in_dim(down_weight, expert_slot, 0, keepdims=False).astype(jnp.float32)

        def add_slice(index, total):
            start = index * slice_width
            block = lax.dynamic_slice_in_dim(hidden, start, slice_width, 1).astype(jnp.float32)
            weights_part = lax.dynamic_slice_in_dim(down, start, slice_width, 0)
            partial_sum = jnp.dot(block, weights_part, precision=lax.Precision.HIGHEST)
            rounded = lax.optimization_barrier(partial_sum.astype(jnp.bfloat16))
            return total + rounded.astype(jnp.float32)
        ffn = lax.fori_loop(0, N_SEQ, add_slice, jnp.zeros((holding * DMAX, D), jnp.float32))
        result = (inputs + ffn.reshape(holding, DMAX, D)).astype(jnp.float32)
        result = result.astype(jnp.bfloat16).astype(jnp.float32)
        result = jnp.where(member[:, None, None], result, jnp.zeros_like(result))
        return (chosen, result)
    chosen_all, results = lax.map(one_expert, jnp.arange(EXPERTS, dtype=jnp.int32))
    row_out = jnp.zeros((TEXT, DMAX, D), jnp.float32).at[chosen_all.reshape(-1)].add(results.reshape(-1, DMAX, D))
    shard_len = durations.astype(jnp.int32)
    ends = jnp.cumsum(shard_len, axis=1).astype(jnp.int32)
    starts = ends - shard_len
    position = jnp.arange(FR_DEV, dtype=jnp.int32)
    row_local = lax.optimization_barrier(jnp.sum((position[None, :, None] >= ends[:, None, :]).astype(jnp.int32), axis=2))
    frame_start = jnp.take_along_axis(starts, row_local, axis=1)
    global_row = jnp.arange(SHARDS, dtype=jnp.int32)[:, None] * R_DEV + row_local
    offsets = position[None, :] - frame_start
    frames = row_out[global_row, offsets]
    return frames.reshape(FRAMES, D).astype(jnp.bfloat16)
```

```python
import functools

import jax
import jax.numpy as jnp
from jax import lax
from jax.experimental import pallas as pl
from jax.experimental.pallas import tpu as pltpu
from jax.sharding import PartitionSpec as P

MESH = pl.DeviceIdType.MESH
FR_DEV = 24
CHUNKS = 2
F32 = jnp.float32
BF16 = jnp.bfloat16


def iota(shape, dim):
    return lax.broadcasted_iota(jnp.int32, shape, dim)


def layer_kernel(
    sizes,
    langs_hbm,
    map_hbm,
    lens_hbm,
    rows_hbm,
    pos_hbm,
    gain_hbm,
    bias_hbm,
    conv_hbm,
    down_hbm,
    out_ref,
    langs_ref,
    map_ref,
    lens_ref,
    rows_ref,
    pos_ref,
    gain_ref,
    bias_ref,
    small_sem,
    conv,
    down,
    send_rows,
    recv_rows,
    rows32,
    chosen,
    chosen_len,
    place,
    frames,
    acc,
    hidden,
    part32,
    own,
    packed,
    from_core,
    from_lang,
    from_seq,
    conv_sem,
    down_sem,
    row_send,
    row_recv,
    core_send,
    core_recv,
    lang_send,
    lang_recv,
    seq_send,
    seq_recv,
):
    n_seq, n_lang, n_panel = sizes
    n = n_seq * n_lang * n_panel
    n_slot = n_lang * n_panel
    rows, width = rows_ref.shape
    slots = pos_ref.shape[0]
    taps = conv.shape[0]
    cap = 2 * rows
    held = cap * n_seq
    block = rows * n_slot
    block_frames = FR_DEV * n_slot
    chunk = width // CHUNKS
    reach = taps // 2
    s = lax.axis_index("seq")
    l = lax.axis_index("lang")
    p = lax.axis_index("panel")
    slot = l * n_panel + p
    me = s * n_slot + slot

    def conv_copy(k):
        return pltpu.make_async_copy(conv_hbm.at[k], conv.at[k], conv_sem.at[k])

    down_copy = pltpu.make_async_copy(down_hbm, down, down_sem)
    small = [
        pltpu.make_async_copy(source, target, small_sem.at[i])
        for i, (source, target) in enumerate(
            [
                (langs_hbm, langs_ref),
                (lens_hbm, lens_ref),
                (rows_hbm, rows_ref),
                (map_hbm, map_ref),
                (pos_hbm, pos_ref),
                (gain_hbm, gain_ref),
                (bias_hbm, bias_ref),
            ]
        )
    ]
    for copy in small[:3]:
        copy.start()

    def peer(step):
        other = lax.rem(me + step, n)
        return other, {
            "seq": other // n_slot,
            "lang": lax.rem(other, n_slot) // n_panel,
            "panel": lax.rem(other, n_panel),
        }

    barrier = pltpu.get_barrier_semaphore()

    def greet(step, carry):
        pl.semaphore_signal(barrier, inc=1, device_id=peer(step)[1], device_id_type=MESH)
        return carry

    lax.fori_loop(1, n, greet, 0, unroll=n - 1 if n <= 16 else 1)
    for copy in small[3:]:
        copy.start()
    for k in range(taps):
        conv_copy(k).start()
    down_copy.start()
    for copy in small[:3]:
        copy.wait()

    row_i, lane_i = iota((rows, 128), 0), iota((rows, 128), 1)
    meta = jnp.zeros((rows, 128), F32)
    for r in range(rows):
        meta = jnp.where((row_i == r) & (lane_i == 0), langs_ref[r].astype(F32), meta)
        meta = jnp.where((row_i == r) & (lane_i == 1), lens_ref[r].astype(F32), meta)
    send_rows[:, :width] = rows_ref[...]
    send_rows[:, width:] = meta.astype(BF16)
    recv_rows[me] = send_rows[...]
    pl.semaphore_wait(barrier, n - 1)

    def row_copy(step, source):
        return pltpu.make_async_remote_copy(
            src_ref=send_rows,
            dst_ref=recv_rows.at[source],
            send_sem=row_send.at[step],
            recv_sem=row_recv.at[source],
            device_id=peer(step)[1],
            device_id_type=MESH,
        )

    def push(step, carry):
        row_copy(step, me).start()
        return carry

    lax.fori_loop(1, n, push, 0, unroll=n - 1 if n <= 16 else 1)
    for copy in small[3:]:
        copy.wait()

    lens_col = meta[:, 1:2]
    r0, r1 = iota((rows, rows), 0), iota((rows, rows), 1)
    own_len = jnp.sum(jnp.where(r0 == r1, lens_col, 0.0), axis=0, keepdims=True)
    own_start = jnp.sum(jnp.where(r0 < r1, lens_col, 0.0), axis=0, keepdims=True)
    f_i = iota((FR_DEV, rows), 0).astype(F32)
    inside = (f_i >= own_start) & (f_i < own_start + own_len)
    inside_f = jnp.where(inside, 1.0, 0.0)
    t_col = jnp.sum(jnp.where(inside, f_i - own_start, 0.0), axis=1, keepdims=True)
    mine32 = rows_ref[...].astype(F32)
    total = jnp.zeros((FR_DEV, width), F32)
    for r in range(rows):
        total = jnp.where(inside_f[:, r : r + 1] > 0.5, mine32[r : r + 1, :], total)
    where_pos = jnp.zeros((FR_DEV, width), F32)
    for t in range(slots):
        where_pos = jnp.where(t_col == float(t), pos_ref[t : t + 1, :], where_pos)
    own[...] = total + where_pos

    zero = jnp.zeros((held, width), BF16)
    for t in range(reach):
        frames[t * held : (t + 1) * held, :] = zero
        frames[(reach + slots + t) * held : (reach + slots + t + 1) * held, :] = zero

    def arrive(step, carry):
        source = lax.rem(me + n - step, n)
        row_copy(step, source).wait_recv()
        return carry

    lax.fori_loop(1, n, arrive, 0)

    def widen(pair, carry):
        two = jnp.concatenate(
            [recv_rows[2 * pair].astype(F32), recv_rows[2 * pair + 1].astype(F32)], axis=0
        )
        rows32[pl.ds(pl.multiple_of(pair * 2 * rows, 2 * rows), 2 * rows), :] = two
        return carry

    lax.fori_loop(0, n // 2, widen, 0, unroll=n // 2 if n <= 16 else 1)

    my_lang = jnp.int32(0)
    for i in range(n_slot):
        my_lang = my_lang + jnp.where(map_ref[i] == slot, i, 0)
    my_lang = my_lang.astype(F32)
    b0, b1 = iota((block, block), 0), iota((block, block), 1)
    same_device = b0 // rows == b1 // rows
    device_start = (iota((1, block), 1) // rows * FR_DEV).astype(F32)
    k_i = iota((cap, block), 0).astype(F32)
    g_i = iota((block_frames, block), 0).astype(F32)
    c_i = iota((block_frames, cap * slots), 1).astype(F32)

    def pick(q, carry):
        part = rows32[pl.ds(pl.multiple_of(q * block, block), block), :]
        lang_col, len_col = part[:, width : width + 1], part[:, width + 1 : width + 2]
        is_mine = jnp.where(lang_col == my_lang, 1.0, 0.0)
        mine_row = jnp.sum(jnp.where(b0 == b1, is_mine, 0.0), axis=0, keepdims=True)
        rank = jnp.sum(jnp.where(b0 < b1, is_mine, 0.0), axis=0, keepdims=True)
        len_row = jnp.sum(jnp.where(b0 == b1, len_col, 0.0), axis=0, keepdims=True)
        start = device_start + jnp.sum(
            jnp.where(same_device & (b0 < b1), len_col, 0.0), axis=0, keepdims=True
        )
        picked = (mine_row > 0.5) & (rank == k_i)
        picked_bf = jnp.where(picked, 1.0, 0.0).astype(BF16)
        at = pl.ds(pl.multiple_of(q * cap, cap), cap)
        chosen[at, :] = jnp.dot(
            picked_bf, part[:, :width].astype(BF16), preferred_element_type=F32
        )
        row_len = jnp.sum(jnp.where(picked, len_row, 0.0), axis=1, keepdims=True)
        chosen_len[at, :] = jnp.broadcast_to(row_len, (cap, 128))
        here = (g_i >= start) & (g_i < start + len_row) & (mine_row > 0.5)
        column = jnp.sum(
            jnp.where(here, (g_i - start) * cap + rank + 1.0, 0.0), axis=1, keepdims=True
        )
        place[q] = jnp.where(c_i + 1.0 == column, 1.0, 0.0).astype(BF16)
        return carry

    lax.fori_loop(0, n_seq, pick, 0, unroll=n_seq if n_seq <= 8 else 1)

    base = chosen[...]
    limit = chosen_len[:, 0:1]
    gain = gain_ref[...]
    for t in range(slots):
        values = base + pos_ref[t : t + 1, :]
        center = values - jnp.mean(values, axis=-1, keepdims=True)
        spread = jnp.mean(center * center, axis=-1, keepdims=True)
        normed = center * lax.rsqrt(spread + 1e-05) * gain
        normed = jnp.where(limit > float(t), normed, 0.0)
        frames[(reach + t) * held : (reach + t + 1) * held, :] = normed.astype(BF16)

    acc[...] = jnp.broadcast_to(bias_ref[...], acc.shape)

    def tap(k, carry):
        conv_copy(k).wait()
        window = frames[pl.ds(pl.multiple_of(k * held, held), held * slots), :]
        acc[...] += jnp.dot(window, conv[k], preferred_element_type=F32)
        return carry

    for k in range(taps):
        conv_copy(k).wait()
        lo, hi = max(0, reach - k), min(slots, slots + reach - k)
        acc[lo * held : hi * held, :] += jnp.dot(
            frames[(k + lo) * held : (k + hi) * held, :], conv[k], preferred_element_type=F32
        )
    pre = acc[...]
    hidden[...] = (0.5 * pre * (1.0 + lax.erf(pre * 0.7071067811865476))).astype(BF16)
    down_copy.wait()

    def core_copy(j, step):
        other = lax.rem(p + step, n_panel)
        source = lax.rem(p + n_panel - step, n_panel)
        return pltpu.make_async_remote_copy(
            src_ref=packed.at[j, other],
            dst_ref=from_core.at[j, step - 1],
            send_sem=core_send.at[j, step - 1],
            recv_sem=core_recv.at[j, step - 1],
            device_id={"panel": other},
            device_id_type=MESH,
        )

    def lang_copy(j, step):
        other = lax.rem(l + step, n_lang)
        return pltpu.make_async_remote_copy(
            src_ref=packed.at[j, p, other],
            dst_ref=from_lang.at[j, step - 1],
            send_sem=lang_send.at[j, step - 1],
            recv_sem=lang_recv.at[j, step - 1],
            device_id={"lang": other},
            device_id_type=MESH,
        )

    def seq_copy(j, step):
        other = lax.rem(s + step, n_seq)
        return pltpu.make_async_remote_copy(
            src_ref=packed.at[j, p, l, other],
            dst_ref=from_seq.at[j, step - 1],
            send_sem=seq_send.at[j, step - 1],
            recv_sem=seq_recv.at[j, step - 1],
            device_id={"seq": other},
            device_id_type=MESH,
        )

    def project(j):
        part = jnp.dot(
            hidden[...],
            down[:, j * chunk : (j + 1) * chunk],
            preferred_element_type=F32,
        )
        part32[...] = part

        def pack(q, carry):
            pieces = [
                part32[pl.ds(pl.multiple_of(t * held + q * cap, cap), cap), :]
                for t in range(slots)
            ]
            mine = jnp.concatenate(pieces, axis=0).astype(BF16)
            moved = jnp.dot(place[q], mine, preferred_element_type=F32)
            for a in range(n_lang):
                for b in range(n_panel):
                    first = (a * n_panel + b) * FR_DEV
                    packed[j, b, a, q] = moved[first : first + FR_DEV, :].astype(BF16)
            return carry

        lax.fori_loop(0, n_seq, pack, 0, unroll=n_seq if n_seq <= 8 else 1)
        for step in range(1, n_panel):
            core_copy(j, step).start()

    def after_core(j):
        for step in range(1, n_panel):
            core_copy(j, step).wait_recv()
            packed[j, p] = packed[j, p] + from_core[j, step - 1]
        for step in range(1, n_lang):
            lang_copy(j, step).start()

    def after_lang(j):
        for step in range(1, n_lang):
            lang_copy(j, step).wait_recv()
            packed[j, p, l] = packed[j, p, l] + from_lang[j, step - 1]

        def go(step, carry):
            seq_copy(j, step).start()
            return carry

        lax.fori_loop(1, n_seq, go, 0)

    def after_seq(j):
        def add(step, total):
            seq_copy(j, step).wait_recv()
            return total + from_seq[j, step - 1].astype(F32)

        ffn = lax.fori_loop(1, n_seq, add, packed[j, p, l, s].astype(F32))
        at = slice(j * chunk, (j + 1) * chunk)
        out_ref[:, at] = (own[:, at] + ffn).astype(BF16)

    for turn in range(CHUNKS + 3):
        if turn < CHUNKS:
            project(turn)
        if 0 <= turn - 1 < CHUNKS:
            after_core(turn - 1)
        if 0 <= turn - 2 < CHUNKS:
            after_lang(turn - 2)
        if 0 <= turn - 3 < CHUNKS:
            after_seq(turn - 3)

    def sent(step, carry):
        row_copy(step, me).wait_send()
        return carry

    lax.fori_loop(1, n, sent, 0)
    for j in range(CHUNKS):
        for step in range(1, n_panel):
            core_copy(j, step).wait_send()
        for step in range(1, n_lang):
            lang_copy(j, step).wait_send()

        def seq_sent(step, carry):
            seq_copy(j, step).wait_send()
            return carry

        lax.fori_loop(1, n_seq, seq_sent, 0)


def per_device(
    sizes,
    text_rows,
    lang_ids,
    lang_map,
    durations,
    pos_table,
    ln_gain,
    conv_weight,
    conv_bias,
    down_weight,
):
    n_seq, n_lang, n_panel = sizes
    n = n_seq * n_lang * n_panel
    rows, width = text_rows.shape
    slots = pos_table.shape[0]
    taps, hidden_width = conv_weight.shape[2], conv_weight.shape[3]
    cap = 2 * rows
    held = cap * n_seq
    n_slot = n_lang * n_panel
    chunk = width // CHUNKS
    dma = pltpu.SemaphoreType.DMA
    vmem = pl.BlockSpec(memory_space=pltpu.VMEM)
    hbm = pl.BlockSpec(memory_space=pl.ANY)
    return pl.pallas_call(
        functools.partial(layer_kernel, sizes),
        out_shape=pltpu.VMEM((FR_DEV, width), BF16),
        in_specs=[hbm] * 9,
        out_specs=vmem,
        scratch_shapes=[
            pltpu.SMEM((rows,), jnp.int32),
            pltpu.SMEM(lang_map.shape, jnp.int32),
            pltpu.SMEM((rows,), jnp.int32),
            pltpu.VMEM((rows, width), BF16),
            pltpu.VMEM((slots, width), F32),
            pltpu.VMEM((1, width), F32),
            pltpu.VMEM((1, hidden_width), F32),
            dma((7,)),
            pltpu.VMEM((taps, width, hidden_width), BF16),
            pltpu.VMEM((hidden_width, width), BF16),
            pltpu.VMEM((rows, width + 128), BF16),
            pltpu.VMEM((n, rows, width + 128), BF16),
            pltpu.VMEM((n * rows, width + 128), F32),
            pltpu.VMEM((held, width), F32),
            pltpu.VMEM((held, 128), F32),
            pltpu.VMEM((n_seq, FR_DEV * n_slot, cap * slots), BF16),
            pltpu.VMEM(((slots + taps - 1) * held, width), BF16),
            pltpu.VMEM((held * slots, hidden_width), F32),
            pltpu.VMEM((held * slots, hidden_width), BF16),
            pltpu.VMEM((held * slots, chunk), F32),
            pltpu.VMEM((FR_DEV, width), F32),
            pltpu.VMEM((CHUNKS, n_panel, n_lang, n_seq, FR_DEV, chunk), BF16),
            pltpu.VMEM((CHUNKS, n_panel - 1, n_lang, n_seq, FR_DEV, chunk), BF16),
            pltpu.VMEM((CHUNKS, n_lang - 1, n_seq, FR_DEV, chunk), BF16),
            pltpu.VMEM((CHUNKS, n_seq - 1, FR_DEV, chunk), BF16),
            dma((taps,)),
            dma(()),
            dma((n,)),
            dma((n,)),
            dma((CHUNKS, n_panel - 1)),
            dma((CHUNKS, n_panel - 1)),
            dma((CHUNKS, n_lang - 1)),
            dma((CHUNKS, n_lang - 1)),
            dma((CHUNKS, n_seq - 1)),
            dma((CHUNKS, n_seq - 1)),
        ],
        compiler_params=pltpu.CompilerParams(
            collective_id=0, has_side_effects=True, vmem_limit_bytes=58 * 1024 * 1024
        ),
    )(
        lang_ids.reshape(rows),
        lang_map,
        durations.reshape(rows),
        text_rows,
        pos_table,
        ln_gain.reshape(1, width),
        conv_bias,
        jnp.transpose(conv_weight[0], (1, 0, 2)),
        down_weight[0],
    )


def solution(mesh):
    sizes = (mesh.shape["seq"], mesh.shape["lang"], mesh.shape["panel"])
    return jax.shard_map(
        functools.partial(per_device, sizes),
        mesh=mesh,
        in_specs=(
            P(("groups", "seq", "lang", "panel"), None),
            P(("groups", "seq", "lang", "panel"), None),
            P(),
            P(("groups", "seq", "lang", "panel"), None),
            P(),
            P(),
            P(("lang", "panel"), None, None, "seq"),
            P(("lang", "panel"), "seq"),
            P(("lang", "panel"), "seq", None),
        ),
        out_specs=P(("groups", "seq", "lang", "panel"), None),
        check_vma=False,
    )
```

```python
import functools

import jax
import jax.numpy as jnp
from jax import lax
from jax.experimental import pallas as pl
from jax.experimental.pallas import tpu as pltpu
from jax.sharding import PartitionSpec as P

MESH = pl.DeviceIdType.MESH
FR_DEV = 24
HALVES = 2
BREAK = 4
F32 = jnp.float32
BF16 = jnp.bfloat16


def iota(shape, dim):
    return lax.broadcasted_iota(jnp.int32, shape, dim)


def layer_kernel(
    sizes,
    langs_hbm,
    map_hbm,
    lens_hbm,
    rows_hbm,
    pos_hbm,
    gain_hbm,
    bias_hbm,
    conv_hbm,
    down_hbm,
    out_ref,
    langs_ref,
    map_ref,
    lens_ref,
    rows_ref,
    pos_ref,
    gain_ref,
    bias_ref,
    small_sem,
    conv,
    down,
    send_rows,
    recv_rows,
    chosen,
    chosen_len,
    place,
    frames,
    acc,
    hidden,
    part32,
    own,
    packed,
    from_core,
    from_lang,
    from_seq,
    conv_sem,
    down_sem,
    row_send,
    row_recv,
    core_send,
    core_recv,
    lang_send,
    lang_recv,
    seq_send,
    seq_recv,
):
    n_seq, n_lang, n_panel = sizes
    n = n_seq * n_lang * n_panel
    n_slot = n_lang * n_panel
    rows, width = rows_ref.shape
    slots = pos_ref.shape[0]
    taps = conv.shape[0]
    cap = 2 * rows
    half = n_seq // HALVES
    held = cap * half
    block = rows * n_slot
    block_frames = FR_DEV * n_slot
    reach = taps // 2
    s = lax.axis_index("seq")
    l = lax.axis_index("lang")
    p = lax.axis_index("panel")
    slot = l * n_panel + p
    me = s * n_slot + slot

    def conv_copy(k):
        return pltpu.make_async_copy(conv_hbm.at[k], conv.at[k], conv_sem.at[k])

    down_copy = pltpu.make_async_copy(down_hbm, down, down_sem)
    small = [
        pltpu.make_async_copy(source, target, small_sem.at[i])
        for i, (source, target) in enumerate(
            [
                (langs_hbm, langs_ref),
                (lens_hbm, lens_ref),
                (rows_hbm, rows_ref),
                (map_hbm, map_ref),
                (pos_hbm, pos_ref),
                (gain_hbm, gain_ref),
                (bias_hbm, bias_ref),
            ]
        )
    ]
    for copy in small[:3]:
        copy.start()

    def peer(step):
        other = lax.rem(me + step, n)
        return other, {
            "seq": other // n_slot,
            "lang": lax.rem(other, n_slot) // n_panel,
            "panel": lax.rem(other, n_panel),
        }

    def for_peers(body):
        if n > 16:
            lax.fori_loop(1, n, lambda step, carry: (body(step), carry)[1], 0)
        else:
            for step in sorted(range(1, n), key=lambda step: -min(step, n - step)):
                body(step)

    barrier = pltpu.get_barrier_semaphore()

    def greet(step):
        pl.semaphore_signal(barrier, inc=1, device_id=peer(step)[1], device_id_type=MESH)

    for_peers(greet)
    for copy in small[3:]:
        copy.start()
    for k in range(taps):
        conv_copy(k).start()
    down_copy.start()
    for copy in small[:3]:
        copy.wait()

    row_i, lane_i = iota((rows, 128), 0), iota((rows, 128), 1)
    meta = jnp.zeros((rows, 128), F32)
    for r in range(rows):
        meta = jnp.where((row_i == r) & (lane_i == 0), langs_ref[r].astype(F32), meta)
        meta = jnp.where((row_i == r) & (lane_i == 1), lens_ref[r].astype(F32), meta)
    send_rows[:, :width] = rows_ref[...]
    send_rows[:, width:] = meta.astype(BF16)
    recv_rows[me] = send_rows[...]
    pl.semaphore_wait(barrier, n - 1)

    def row_copy(step, source):
        return pltpu.make_async_remote_copy(
            src_ref=send_rows,
            dst_ref=recv_rows.at[source],
            send_sem=row_send.at[step],
            recv_sem=row_recv.at[source],
            device_id=peer(step)[1],
            device_id_type=MESH,
        )

    for_peers(lambda step: row_copy(step, me).start())
    for copy in small[3:]:
        copy.wait()

    lens_col = meta[:, 1:2]
    r0, r1 = iota((rows, rows), 0), iota((rows, rows), 1)
    own_len = jnp.sum(jnp.where(r0 == r1, lens_col, 0.0), axis=0, keepdims=True)
    own_start = jnp.sum(jnp.where(r0 < r1, lens_col, 0.0), axis=0, keepdims=True)
    f_i = iota((FR_DEV, rows), 0).astype(F32)
    inside = (f_i >= own_start) & (f_i < own_start + own_len)
    inside_f = jnp.where(inside, 1.0, 0.0)
    t_col = jnp.sum(jnp.where(inside, f_i - own_start, 0.0), axis=1, keepdims=True)
    mine32 = rows_ref[...].astype(F32)
    total = jnp.zeros((FR_DEV, width), F32)
    for r in range(rows):
        total = jnp.where(inside_f[:, r : r + 1] > 0.5, mine32[r : r + 1, :], total)
    where_pos = jnp.zeros((FR_DEV, width), F32)
    for t in range(slots):
        where_pos = jnp.where(t_col == float(t), pos_ref[t : t + 1, :], where_pos)
    own[...] = total + where_pos

    zero = jnp.zeros((reach * held, width), BF16)
    for g in range(HALVES):
        frames[g, : reach * held, :] = zero
        frames[g, (reach + slots) * held :, :] = zero

    order = sorted(range(n_seq), key=lambda step: -min(step, n_seq - step))

    def for_part(first, last, body):
        if n_seq > 8:
            lax.fori_loop(
                first,
                last,
                lambda j, carry: (body(j, lax.rem(j + 1, n_seq)), carry)[1],
                0,
            )
        else:
            for j in range(first, last):
                body(j, order[j])

    def to_seq(step):
        return lax.rem(s + step, n_seq)

    for_peers(lambda step: row_copy(step, lax.rem(me + n - step, n)).wait_recv())

    my_lang = jnp.int32(0)
    for i in range(n_slot):
        my_lang = my_lang + jnp.where(map_ref[i] == slot, i, 0)
    my_lang = my_lang.astype(F32)
    b0, b1 = iota((block, block), 0), iota((block, block), 1)
    same_device = b0 // rows == b1 // rows
    device_start = (iota((1, block), 1) // rows * FR_DEV).astype(F32)
    k_i = iota((cap, block), 0).astype(F32)
    g_i = iota((block_frames, block), 0).astype(F32)
    c_i = iota((block_frames, cap * slots), 1).astype(F32)

    def pick(j, step):
        q = to_seq(step)
        part = jnp.concatenate(
            [recv_rows[q * n_slot + i].astype(F32) for i in range(n_slot)], axis=0
        )
        lang_col, len_col = part[:, width : width + 1], part[:, width + 1 : width + 2]
        is_mine = jnp.where(lang_col == my_lang, 1.0, 0.0)
        mine_row = jnp.sum(jnp.where(b0 == b1, is_mine, 0.0), axis=0, keepdims=True)
        rank = jnp.sum(jnp.where(b0 < b1, is_mine, 0.0), axis=0, keepdims=True)
        len_row = jnp.sum(jnp.where(b0 == b1, len_col, 0.0), axis=0, keepdims=True)
        start = device_start + jnp.sum(
            jnp.where(same_device & (b0 < b1), len_col, 0.0), axis=0, keepdims=True
        )
        picked = (mine_row > 0.5) & (rank == k_i)
        picked_bf = jnp.where(picked, 1.0, 0.0).astype(BF16)
        at = pl.ds(pl.multiple_of(j * cap, cap), cap)
        chosen[at, :] = jnp.dot(
            picked_bf, part[:, :width].astype(BF16), preferred_element_type=F32
        )
        row_len = jnp.sum(jnp.where(picked, len_row, 0.0), axis=1, keepdims=True)
        chosen_len[at, :] = jnp.broadcast_to(row_len, (cap, 128))
        here = (g_i >= start) & (g_i < start + len_row) & (mine_row > 0.5)
        column = jnp.sum(
            jnp.where(here, (g_i - start) * cap + rank + 1.0, 0.0), axis=1, keepdims=True
        )
        place[j] = jnp.where(c_i + 1.0 == column, 1.0, 0.0).astype(BF16)

    for_part(0, n_seq, pick)

    gain = gain_ref[...]

    def normalize(g):
        base = chosen[g * held : (g + 1) * held, :]
        limit = chosen_len[g * held : (g + 1) * held, 0:1]
        for t in range(slots):
            values = base + pos_ref[t : t + 1, :]
            center = values - jnp.mean(values, axis=-1, keepdims=True)
            spread = jnp.mean(center * center, axis=-1, keepdims=True)
            normed = center * lax.rsqrt(spread + 1e-05) * gain
            normed = jnp.where(limit > float(t), normed, 0.0)
            frames[g, (reach + t) * held : (reach + t + 1) * held, :] = normed.astype(BF16)

    def convolve(g, first, last):
        if g == 0:
            for k in range(first, last):
                conv_copy(k).wait()
        for k in range(first, last):
            term = jnp.dot(
                frames[g, k * held : (k + slots) * held, :],
                conv[k],
                preferred_element_type=F32,
            )
            acc[g] = term + (bias_ref[...] if k == 0 else acc[g])

    def project(g):
        pre = acc[g]
        act = 0.5 * pre * (1.0 + lax.erf(pre * 0.7071067811865476))
        hidden[g] = act.astype(BF16)
        if g == 0:
            down_copy.wait()
        part32[g] = jnp.dot(hidden[g], down[...], preferred_element_type=F32)

    other_core = lax.rem(p + 1, n_panel)

    def core_copy(j, step):
        return pltpu.make_async_remote_copy(
            src_ref=packed.at[to_seq(step), other_core],
            dst_ref=from_core.at[j],
            send_sem=core_send.at[j],
            recv_sem=core_recv.at[j],
            device_id={"panel": other_core},
            device_id_type=MESH,
        )

    def lang_copy(j, step, turn):
        other = lax.rem(l + turn, n_lang)
        return pltpu.make_async_remote_copy(
            src_ref=packed.at[to_seq(step), p, other],
            dst_ref=from_lang.at[j, turn - 1],
            send_sem=lang_send.at[j, turn - 1],
            recv_sem=lang_recv.at[j, turn - 1],
            device_id={"lang": other},
            device_id_type=MESH,
        )

    def seq_copy(j, step):
        other = to_seq(step)
        return pltpu.make_async_remote_copy(
            src_ref=packed.at[other, p, l],
            dst_ref=from_seq.at[j],
            send_sem=seq_send.at[j],
            recv_sem=seq_recv.at[j],
            device_id={"seq": other},
            device_id_type=MESH,
        )

    def pack(g, j, step):
        q = to_seq(step)
        pieces = [
            part32[g, pl.ds(pl.multiple_of(t * held + (j - g * half) * cap, cap), cap), :]
            for t in range(slots)
        ]
        mine = jnp.concatenate(pieces, axis=0).astype(BF16)
        moved = jnp.dot(place[j], mine, preferred_element_type=F32).astype(BF16)
        for a in range(n_lang):
            for b in range(n_panel):
                first = (a * n_panel + b) * FR_DEV
                packed[q, b, a] = moved[first : first + FR_DEV, :]
        core_copy(j, step).start()

    def after_core(j, step):
        core_copy(j, step).wait_recv()
        q = to_seq(step)
        packed[q, p] = packed[q, p] + from_core[j]
        for turn in range(1, n_lang):
            lang_copy(j, step, turn).start()

    def add_lang(j, step):
        total = packed[to_seq(step), p, l]
        for turn in range(1, n_lang):
            lang_copy(j, step, turn).wait_recv()
            total = total + from_lang[j, turn - 1]
        return total

    def after_lang(j, step):
        packed[to_seq(step), p, l] = add_lang(j, step)
        seq_copy(j, step).start()

    normalize(0)
    convolve(0, 0, taps)
    project(0)
    for_part(0, half, functools.partial(pack, 0))
    normalize(1)
    convolve(1, 0, BREAK)
    for_part(0, half, after_core)
    convolve(1, BREAK, taps)
    project(1)
    for_part(half, n_seq, functools.partial(pack, 1))
    for_part(0, half, after_lang)
    for_part(half, n_seq, after_core)
    for_part(half, n_seq - 1, after_lang)
    own[...] += add_lang(n_seq - 1, 0).astype(F32)

    def after_seq(j, step):
        seq_copy(j, step).wait_recv()
        own[...] += from_seq[j].astype(F32)

    for_part(0, n_seq - 1, after_seq)
    out_ref[...] = own[...].astype(BF16)

    def sent(j, step):
        core_copy(j, step).wait_send()
        for turn in range(1, n_lang):
            lang_copy(j, step, turn).wait_send()

    for_peers(lambda step: row_copy(step, me).wait_send())
    for_part(0, n_seq, sent)
    for_part(0, n_seq - 1, lambda j, step: seq_copy(j, step).wait_send())


def per_device(
    sizes,
    text_rows,
    lang_ids,
    lang_map,
    durations,
    pos_table,
    ln_gain,
    conv_weight,
    conv_bias,
    down_weight,
):
    n_seq, n_lang, n_panel = sizes
    n = n_seq * n_lang * n_panel
    rows, width = text_rows.shape
    slots = pos_table.shape[0]
    taps, hidden_width = conv_weight.shape[2], conv_weight.shape[3]
    cap = 2 * rows
    held = cap * n_seq
    n_slot = n_lang * n_panel
    dma = pltpu.SemaphoreType.DMA
    vmem = pl.BlockSpec(memory_space=pltpu.VMEM)
    hbm = pl.BlockSpec(memory_space=pl.ANY)
    return pl.pallas_call(
        functools.partial(layer_kernel, sizes),
        out_shape=pltpu.VMEM((FR_DEV, width), BF16),
        in_specs=[hbm] * 9,
        out_specs=vmem,
        scratch_shapes=[
            pltpu.SMEM((rows,), jnp.int32),
            pltpu.SMEM(lang_map.shape, jnp.int32),
            pltpu.SMEM((rows,), jnp.int32),
            pltpu.VMEM((rows, width), BF16),
            pltpu.VMEM((slots, width), F32),
            pltpu.VMEM((1, width), F32),
            pltpu.VMEM((1, hidden_width), F32),
            dma((7,)),
            pltpu.VMEM((taps, width, hidden_width), BF16),
            pltpu.VMEM((hidden_width, width), BF16),
            pltpu.VMEM((rows, width + 128), BF16),
            pltpu.VMEM((n, rows, width + 128), BF16),
            pltpu.VMEM((held, width), F32),
            pltpu.VMEM((held, 128), F32),
            pltpu.VMEM((n_seq, FR_DEV * n_slot, cap * slots), BF16),
            pltpu.VMEM((HALVES, (slots + taps - 1) * held // HALVES, width), BF16),
            pltpu.VMEM((HALVES, held * slots // HALVES, hidden_width), F32),
            pltpu.VMEM((HALVES, held * slots // HALVES, hidden_width), BF16),
            pltpu.VMEM((HALVES, held * slots // HALVES, width), F32),
            pltpu.VMEM((FR_DEV, width), F32),
            pltpu.VMEM((n_seq, n_panel, n_lang, FR_DEV, width), BF16),
            pltpu.VMEM((n_seq, n_lang, FR_DEV, width), BF16),
            pltpu.VMEM((n_seq, n_lang - 1, FR_DEV, width), BF16),
            pltpu.VMEM((n_seq - 1, FR_DEV, width), BF16),
            dma((taps,)),
            dma(()),
            dma((n,)),
            dma((n,)),
            dma((n_seq,)),
            dma((n_seq,)),
            dma((n_seq, n_lang - 1)),
            dma((n_seq, n_lang - 1)),
            dma((n_seq - 1,)),
            dma((n_seq - 1,)),
        ],
        compiler_params=pltpu.CompilerParams(
            collective_id=0, has_side_effects=True, vmem_limit_bytes=58 * 1024 * 1024
        ),
    )(
        lang_ids.reshape(rows),
        lang_map,
        durations.reshape(rows),
        text_rows,
        pos_table,
        ln_gain.reshape(1, width),
        conv_bias,
        jnp.transpose(conv_weight[0], (1, 0, 2)),
        down_weight[0],
    )


def solution(mesh):
    sizes = (mesh.shape["seq"], mesh.shape["lang"], mesh.shape["panel"])
    return jax.shard_map(
        functools.partial(per_device, sizes),
        mesh=mesh,
        in_specs=(
            P(("groups", "seq", "lang", "panel"), None),
            P(("groups", "seq", "lang", "panel"), None),
            P(),
            P(("groups", "seq", "lang", "panel"), None),
            P(),
            P(),
            P(("lang", "panel"), None, None, "seq"),
            P(("lang", "panel"), "seq"),
            P(("lang", "panel"), "seq", None),
        ),
        out_specs=P(("groups", "seq", "lang", "panel"), None),
        check_vma=False,
    )
```

```python
import functools

import jax
import jax.numpy as jnp
from jax import lax
from jax.experimental import pallas as pl
from jax.experimental.pallas import tpu as pltpu
from jax.sharding import PartitionSpec as P

MESH = pl.DeviceIdType.MESH
FR_DEV = 24
HALVES = 2
BREAK = 3
PARTS = 2
DIRECT = (1,2)
F32 = jnp.float32
BF16 = jnp.bfloat16


def iota(shape, dim):
    return lax.broadcasted_iota(jnp.int32, shape, dim)


def layer_kernel(
    sizes,
    langs_hbm,
    map_hbm,
    lens_hbm,
    rows_hbm,
    pos_hbm,
    gain_hbm,
    bias_hbm,
    conv_hbm,
    down_hbm,
    out_ref,
    langs_ref,
    map_ref,
    lens_ref,
    rows_ref,
    pos_ref,
    gain_ref,
    bias_ref,
    small_sem,
    conv,
    down,
    send_rows,
    recv_rows,
    chosen,
    chosen_len,
    place,
    frames,
    acc,
    hidden,
    part32,
    own,
    packed,
    from_core,
    from_lang,
    from_seq,
    conv_sem,
    down_sem,
    row_send,
    row_recv,
    pass_send,
    pass_recv,
    core_send,
    core_recv,
    lang_send,
    lang_recv,
    seq_send,
    seq_recv,
):
    n_seq, n_lang, n_panel = sizes
    n_slot = n_lang * n_panel
    rows, width = rows_ref.shape
    slots = pos_ref.shape[0]
    taps = conv.shape[0]
    cap = 2 * rows
    half = n_seq // HALVES
    held = cap * half
    block = rows * n_slot
    block_frames = FR_DEV * n_slot
    reach = taps // 2
    s = lax.axis_index("seq")
    l = lax.axis_index("lang")
    p = lax.axis_index("panel")
    slot = l * n_panel + p
    chips = n_seq * n_lang
    chip = s * n_lang + l
    other_core = lax.rem(p + 1, n_panel)

    def conv_copy(k):
        return pltpu.make_async_copy(conv_hbm.at[k], conv.at[k], conv_sem.at[k])

    down_copy = pltpu.make_async_copy(down_hbm, down, down_sem)
    small = [
        pltpu.make_async_copy(source, target, small_sem.at[i])
        for i, (source, target) in enumerate(
            [
                (langs_hbm, langs_ref),
                (lens_hbm, lens_ref),
                (rows_hbm, rows_ref),
                (map_hbm, map_ref),
                (pos_hbm, pos_ref),
                (gain_hbm, gain_ref),
                (bias_hbm, bias_ref),
            ]
        )
    ]
    for copy in small[:3]:
        copy.start()

    small_mesh = (n_seq, n_lang, n_panel) == (4, 2, 2)
    order = [2, 3, 1, 0] if small_mesh else list(range(n_seq))
    direct = DIRECT if small_mesh else ()

    def is_direct(j):
        return isinstance(j, int) and j in direct

    def flip(index, bits):
        other = index
        for bit in (1, 2):
            if bits & bit:
                other = other + bit - 2 * bit * lax.rem(index // bit, 2)
        return other

    def to_seq(step):
        return flip(s, step) if small_mesh else lax.rem(s + step, n_seq)

    def peer(step):
        if small_mesh:
            at = (flip(s, step // 2), flip(l, step % 2))
            return at[0] * n_lang + at[1], {"seq": at[0], "lang": at[1]}
        other = lax.rem(chip + step, chips)
        return other, {"seq": other // n_lang, "lang": lax.rem(other, n_lang)}

    def from_peer(step):
        return peer(step)[0] if small_mesh else lax.rem(chip + chips - step, chips)

    def for_peers(body, first=1, last=chips):
        if small_mesh:
            for step in reversed(range(first, last)):
                body(step)
        else:
            lax.fori_loop(first, last, lambda step, carry: (body(step), carry)[1], 0)

    def for_part(first, last, body):
        if small_mesh:
            for j in range(first, last):
                body(j, order[j])
        else:
            lax.fori_loop(
                first,
                last,
                lambda j, carry: (body(j, lax.rem(j + 1, n_seq)), carry)[1],
                0,
            )

    barrier = pltpu.get_barrier_semaphore()

    def greet(step):
        pl.semaphore_signal(barrier, inc=1, device_id=peer(step)[1], device_id_type=MESH)

    for_peers(greet)
    pl.semaphore_signal(
        barrier, inc=1, device_id={"panel": other_core}, device_id_type=MESH
    )
    for copy in small[3:]:
        copy.start()
    for k in range(taps):
        conv_copy(k).start()
    down_copy.start()
    for copy in small[:3]:
        copy.wait()

    row_i, lane_i = iota((rows, 128), 0), iota((rows, 128), 1)
    meta = jnp.zeros((rows, 128), F32)
    for r in range(rows):
        meta = jnp.where((row_i == r) & (lane_i == 0), langs_ref[r].astype(F32), meta)
        meta = jnp.where((row_i == r) & (lane_i == 1), lens_ref[r].astype(F32), meta)
    send_rows[:, :width] = rows_ref[...]
    send_rows[:, width:] = meta.astype(BF16)
    recv_rows[p, chip] = send_rows[...]
    pl.semaphore_wait(barrier, chips)

    def row_copy(step, source):
        return pltpu.make_async_remote_copy(
            src_ref=send_rows,
            dst_ref=recv_rows.at[p, source],
            send_sem=row_send.at[step],
            recv_sem=row_recv.at[source],
            device_id=peer(step)[1],
            device_id_type=MESH,
        )

    for_peers(lambda step: row_copy(step, chip).start())

    spans = PARTS if small_mesh else 1
    span = chips // spans

    def pass_copy(which):
        at = pl.ds((s // 2 if which == 0 else 1 - s // 2) * span if spans == 2 else 0, span)
        return pltpu.make_async_remote_copy(
            src_ref=recv_rows.at[p, at],
            dst_ref=recv_rows.at[p, at],
            send_sem=pass_send.at[which],
            recv_sem=pass_recv.at[which],
            device_id={"panel": other_core},
            device_id_type=MESH,
        )

    def pass_arrival(which):
        at = pl.ds((s // 2 if which == 0 else 1 - s // 2) * span if spans == 2 else 0, span)
        return pltpu.make_async_remote_copy(
            src_ref=recv_rows.at[other_core, at],
            dst_ref=recv_rows.at[other_core, at],
            send_sem=pass_send.at[which],
            recv_sem=pass_recv.at[which],
            device_id={"panel": other_core},
            device_id_type=MESH,
        )

    for copy in small[3:]:
        copy.wait()

    lens_col = meta[:, 1:2]
    r0, r1 = iota((rows, rows), 0), iota((rows, rows), 1)
    own_len = jnp.sum(jnp.where(r0 == r1, lens_col, 0.0), axis=0, keepdims=True)
    own_start = jnp.sum(jnp.where(r0 < r1, lens_col, 0.0), axis=0, keepdims=True)
    f_i = iota((FR_DEV, rows), 0).astype(F32)
    inside = (f_i >= own_start) & (f_i < own_start + own_len)
    inside_f = jnp.where(inside, 1.0, 0.0)
    t_col = jnp.sum(jnp.where(inside, f_i - own_start, 0.0), axis=1, keepdims=True)
    mine32 = rows_ref[...].astype(F32)
    total = jnp.zeros((FR_DEV, width), F32)
    for r in range(rows):
        total = jnp.where(inside_f[:, r : r + 1] > 0.5, mine32[r : r + 1, :], total)
    where_pos = jnp.zeros((FR_DEV, width), F32)
    for t in range(slots):
        where_pos = jnp.where(t_col == float(t), pos_ref[t : t + 1, :], where_pos)
    own[...] = total + where_pos

    zero = jnp.zeros((reach * held, width), BF16)
    for g in range(HALVES):
        frames[g, : reach * held, :] = zero
        frames[g, (reach + slots) * held :, :] = zero

    order = list(range(n_seq - 1, -1, -1))
    if n_seq == 4:
        order = [2, 3, 1, 0]
    direct = DIRECT if n_seq == 4 else ()

    def for_part(first, last, body):
        if n_seq > 8:
            lax.fori_loop(
                first,
                last,
                lambda j, carry: (body(j, lax.rem(j + 1, n_seq)), carry)[1],
                0,
            )
        else:
            for j in range(first, last):
                body(j, order[j])


    my_lang = jnp.int32(0)
    for i in range(n_slot):
        my_lang = my_lang + jnp.where(map_ref[i] == slot, i, 0)
    my_lang = my_lang.astype(F32)
    b0, b1 = iota((block, block), 0), iota((block, block), 1)
    same_device = b0 // rows == b1 // rows
    device_start = (iota((1, block), 1) // rows * FR_DEV).astype(F32)
    k_i = iota((cap, block), 0).astype(F32)
    g_i = iota((block_frames, block), 0).astype(F32)
    c_i = iota((block_frames, cap * slots), 1).astype(F32)

    def pick(j, step):
        q = to_seq(step)
        part = jnp.concatenate(
            [
                recv_rows[b, q * n_lang + a].astype(F32)
                for a in range(n_lang)
                for b in range(n_panel)
            ],
            axis=0,
        )
        lang_col, len_col = part[:, width : width + 1], part[:, width + 1 : width + 2]
        is_mine = jnp.where(lang_col == my_lang, 1.0, 0.0)
        mine_row = jnp.sum(jnp.where(b0 == b1, is_mine, 0.0), axis=0, keepdims=True)
        rank = jnp.sum(jnp.where(b0 < b1, is_mine, 0.0), axis=0, keepdims=True)
        len_row = jnp.sum(jnp.where(b0 == b1, len_col, 0.0), axis=0, keepdims=True)
        start = device_start + jnp.sum(
            jnp.where(same_device & (b0 < b1), len_col, 0.0), axis=0, keepdims=True
        )
        picked = (mine_row > 0.5) & (rank == k_i)
        picked_bf = jnp.where(picked, 1.0, 0.0).astype(BF16)
        at = pl.ds(pl.multiple_of(j * cap, cap), cap)
        chosen[at, :] = jnp.dot(
            picked_bf, part[:, :width].astype(BF16), preferred_element_type=F32
        )
        row_len = jnp.sum(jnp.where(picked, len_row, 0.0), axis=1, keepdims=True)
        chosen_len[at, :] = jnp.broadcast_to(row_len, (cap, 128))
        here = (g_i >= start) & (g_i < start + len_row) & (mine_row > 0.5)
        column = jnp.sum(
            jnp.where(here, (g_i - start) * cap + rank + 1.0, 0.0), axis=1, keepdims=True
        )
        place[j] = jnp.where(c_i + 1.0 == column, 1.0, 0.0).astype(BF16)


    gain = gain_ref[...]

    def normalize(g):
        base = chosen[g * held : (g + 1) * held, :]
        limit = chosen_len[g * held : (g + 1) * held, 0:1]
        for t in range(slots):
            values = base + pos_ref[t : t + 1, :]
            center = values - jnp.mean(values, axis=-1, keepdims=True)
            spread = jnp.mean(center * center, axis=-1, keepdims=True)
            normed = center * lax.rsqrt(spread + 1e-05) * gain
            normed = jnp.where(limit > float(t), normed, 0.0)
            frames[g, (reach + t) * held : (reach + t + 1) * held, :] = normed.astype(BF16)

    def convolve(g, first, last):
        if g == 0:
            for k in range(first, last):
                conv_copy(k).wait()
        for k in range(first, last):
            term = jnp.dot(
                frames[g, k * held : (k + slots) * held, :],
                conv[k],
                preferred_element_type=F32,
            )
            acc[g] = term + (bias_ref[...] if k == 0 else acc[g])

    def project(g):
        pre = acc[g]
        act = 0.5 * pre * (1.0 + lax.erf(pre * 0.7071067811865476))
        hidden[g] = act.astype(BF16)
        if g == 0:
            down_copy.wait()
        part32[g] = jnp.dot(hidden[g], down[...], preferred_element_type=F32)

    def core_copy(j, step):
        return pltpu.make_async_remote_copy(
            src_ref=packed.at[to_seq(step), other_core],
            dst_ref=from_core.at[j],
            send_sem=core_send.at[j],
            recv_sem=core_recv.at[j],
            device_id={"panel": other_core},
            device_id_type=MESH,
        )

    def lang_copy(j, step, turn):
        other = lax.rem(l + turn, n_lang)
        return pltpu.make_async_remote_copy(
            src_ref=packed.at[to_seq(step), p, other],
            dst_ref=from_lang.at[j, turn - 1],
            send_sem=lang_send.at[j, turn - 1],
            recv_sem=lang_recv.at[j, turn - 1],
            device_id={"lang": other, "seq": to_seq(step)} if is_direct(j) else {"lang": other},
            device_id_type=MESH,
        )

    def seq_copy(j, step):
        other = to_seq(step)
        return pltpu.make_async_remote_copy(
            src_ref=packed.at[other, p, l],
            dst_ref=from_seq.at[j],
            send_sem=seq_send.at[j],
            recv_sem=seq_recv.at[j],
            device_id={"seq": other},
            device_id_type=MESH,
        )

    def pack(g, j, step):
        q = to_seq(step)
        pieces = [
            part32[g, pl.ds(pl.multiple_of(t * held + (j - g * half) * cap, cap), cap), :]
            for t in range(slots)
        ]
        mine = jnp.concatenate(pieces, axis=0).astype(BF16)
        moved = jnp.dot(place[j], mine, preferred_element_type=F32).astype(BF16)
        for a in range(n_lang):
            for b in range(n_panel):
                first = (a * n_panel + b) * FR_DEV
                packed[q, b, a] = moved[first : first + FR_DEV, :]
        core_copy(j, step).start()

    def after_core(j, step):
        core_copy(j, step).wait_recv()
        q = to_seq(step)
        packed[q, p] = packed[q, p] + from_core[j]
        for turn in range(1, n_lang):
            lang_copy(j, step, turn).start()
        if is_direct(j):
            seq_copy(j, step).start()

    def add_lang(j, step):
        total = packed[to_seq(step), p, l]
        for turn in range(1, n_lang):
            lang_copy(j, step, turn).wait_recv()
            total = total + from_lang[j, turn - 1]
        return total

    def after_lang(j, step):
        if is_direct(j):
            return
        packed[to_seq(step), p, l] = add_lang(j, step)
        seq_copy(j, step).start()

    def arrive(first, last):
        for_peers(lambda step: row_copy(step, from_peer(step)).wait_recv(), first, last)

    if spans == 2:
        arrive(1, span)
        pass_copy(0).start()
        arrive(span, chips)
        pass_copy(1).start()
        pass_arrival(0).wait_recv()
        for_part(half, n_seq, pick)
        normalize(1)
        pass_arrival(1).wait_recv()
        for_part(0, half, pick)
        normalize(0)
    else:
        arrive(1, chips)
        pass_copy(0).start()
        pass_arrival(0).wait_recv()
        for_part(0, n_seq, pick)
        normalize(0)
        normalize(1)
    convolve(0, 0, taps)
    project(0)
    for_part(0, half, functools.partial(pack, 0))
    convolve(1, 0, BREAK)
    for_part(0, half, after_core)
    convolve(1, BREAK, taps)
    project(1)
    for_part(half, n_seq, functools.partial(pack, 1))
    for_part(0, half, after_lang)
    for_part(half, n_seq, after_core)
    for_part(half, n_seq - 1, after_lang)
    own[...] += add_lang(n_seq - 1, 0).astype(F32)

    def after_seq(j, step):
        seq_copy(j, step).wait_recv()
        total = own[...] + from_seq[j].astype(F32)
        if is_direct(j):
            for turn in range(1, n_lang):
                lang_copy(j, step, turn).wait_recv()
                total = total + from_lang[j, turn - 1].astype(F32)
        own[...] = total

    for_part(0, n_seq - 1, after_seq)
    out_ref[...] = own[...].astype(BF16)

    def sent(j, step):
        core_copy(j, step).wait_send()
        for turn in range(1, n_lang):
            lang_copy(j, step, turn).wait_send()

    for_peers(lambda step: row_copy(step, chip).wait_send())
    for which in range(spans):
        pass_copy(which).wait_send()
    for_part(0, n_seq, sent)
    for_part(0, n_seq - 1, lambda j, step: seq_copy(j, step).wait_send())


def per_device(
    sizes,
    text_rows,
    lang_ids,
    lang_map,
    durations,
    pos_table,
    ln_gain,
    conv_weight,
    conv_bias,
    down_weight,
):
    n_seq, n_lang, n_panel = sizes
    chips = n_seq * n_lang
    rows, width = text_rows.shape
    slots = pos_table.shape[0]
    taps, hidden_width = conv_weight.shape[2], conv_weight.shape[3]
    cap = 2 * rows
    held = cap * n_seq
    n_slot = n_lang * n_panel
    dma = pltpu.SemaphoreType.DMA
    vmem = pl.BlockSpec(memory_space=pltpu.VMEM)
    hbm = pl.BlockSpec(memory_space=pl.ANY)
    return pl.pallas_call(
        functools.partial(layer_kernel, sizes),
        out_shape=pltpu.VMEM((FR_DEV, width), BF16),
        in_specs=[hbm] * 9,
        out_specs=vmem,
        scratch_shapes=[
            pltpu.SMEM((rows,), jnp.int32),
            pltpu.SMEM(lang_map.shape, jnp.int32),
            pltpu.SMEM((rows,), jnp.int32),
            pltpu.VMEM((rows, width), BF16),
            pltpu.VMEM((slots, width), F32),
            pltpu.VMEM((1, width), F32),
            pltpu.VMEM((1, hidden_width), F32),
            dma((7,)),
            pltpu.VMEM((taps, width, hidden_width), BF16),
            pltpu.VMEM((hidden_width, width), BF16),
            pltpu.VMEM((rows, width + 128), BF16),
            pltpu.VMEM((n_panel, chips, rows, width + 128), BF16),
            pltpu.VMEM((held, width), F32),
            pltpu.VMEM((held, 128), F32),
            pltpu.VMEM((n_seq, FR_DEV * n_slot, cap * slots), BF16),
            pltpu.VMEM((HALVES, (slots + taps - 1) * held // HALVES, width), BF16),
            pltpu.VMEM((HALVES, held * slots // HALVES, hidden_width), F32),
            pltpu.VMEM((HALVES, held * slots // HALVES, hidden_width), BF16),
            pltpu.VMEM((HALVES, held * slots // HALVES, width), F32),
            pltpu.VMEM((FR_DEV, width), F32),
            pltpu.VMEM((n_seq, n_panel, n_lang, FR_DEV, width), BF16),
            pltpu.VMEM((n_seq, n_lang, FR_DEV, width), BF16),
            pltpu.VMEM((n_seq, n_lang - 1, FR_DEV, width), BF16),
            pltpu.VMEM((n_seq - 1, FR_DEV, width), BF16),
            dma((taps,)),
            dma(()),
            dma((chips,)),
            dma((chips,)),
            dma((PARTS,)),
            dma((PARTS,)),
            dma((n_seq,)),
            dma((n_seq,)),
            dma((n_seq, n_lang - 1)),
            dma((n_seq, n_lang - 1)),
            dma((n_seq - 1,)),
            dma((n_seq - 1,)),
        ],
        compiler_params=pltpu.CompilerParams(
            collective_id=0, has_side_effects=True, vmem_limit_bytes=58 * 1024 * 1024
        ),
    )(
        lang_ids.reshape(rows),
        lang_map,
        durations.reshape(rows),
        text_rows,
        pos_table,
        ln_gain.reshape(1, width),
        conv_bias,
        jnp.transpose(conv_weight[0], (1, 0, 2)),
        down_weight[0],
    )


def solution(mesh):
    sizes = (mesh.shape["seq"], mesh.shape["lang"], mesh.shape["panel"])
    return jax.shard_map(
        functools.partial(per_device, sizes),
        mesh=mesh,
        in_specs=(
            P(("groups", "seq", "lang", "panel"), None),
            P(("groups", "seq", "lang", "panel"), None),
            P(),
            P(("groups", "seq", "lang", "panel"), None),
            P(),
            P(),
            P(("lang", "panel"), None, None, "seq"),
            P(("lang", "panel"), "seq"),
            P(("lang", "panel"), "seq", None),
        ),
        out_specs=P(("groups", "seq", "lang", "panel"), None),
        check_vma=False,
    )
```

```python
import functools

import jax
import jax.numpy as jnp
from jax import lax
from jax.experimental import pallas as pl
from jax.experimental.pallas import tpu as pltpu
from jax.sharding import PartitionSpec as P

MESH = pl.DeviceIdType.MESH
FR_DEV = 24
HALVES = 2
BREAK = 4
PARTS = 2
SPLITS = ((0, 1024), (1024,), (0, 1024), (1024,))
F32 = jnp.float32
BF16 = jnp.bfloat16


def iota(shape, dim):
    return lax.broadcasted_iota(jnp.int32, shape, dim)


def layer_kernel(
    sizes,
    langs_hbm,
    map_hbm,
    lens_hbm,
    rows_hbm,
    pos_hbm,
    gain_hbm,
    bias_hbm,
    conv_hbm,
    down_hbm,
    out_ref,
    langs_ref,
    map_ref,
    lens_ref,
    rows_ref,
    pos_ref,
    gain_ref,
    bias_ref,
    small_sem,
    conv,
    down,
    send_rows,
    recv_rows,
    chosen,
    chosen_len,
    place,
    frames,
    acc,
    hidden,
    part32,
    own,
    packed,
    from_core,
    from_lang,
    from_seq,
    conv_sem,
    down_sem,
    row_send,
    row_recv,
    pass_send,
    pass_recv,
    core_send,
    core_recv,
    lang_send,
    lang_recv,
    seq_send,
    seq_recv,
):
    n_seq, n_lang, n_panel = sizes
    n_slot = n_lang * n_panel
    rows, width = rows_ref.shape
    slots = pos_ref.shape[0]
    taps = conv.shape[0]
    cap = 2 * rows
    half = n_seq // HALVES
    held = cap * half
    block = rows * n_slot
    block_frames = FR_DEV * n_slot
    reach = taps // 2
    s = lax.axis_index("seq")
    l = lax.axis_index("lang")
    p = lax.axis_index("panel")
    slot = l * n_panel + p
    chips = n_seq * n_lang
    chip = s * n_lang + l
    other_core = lax.rem(p + 1, n_panel)

    def conv_copy(k):
        return pltpu.make_async_copy(conv_hbm.at[k], conv.at[k], conv_sem.at[k])

    down_copy = pltpu.make_async_copy(down_hbm, down, down_sem)
    small = [
        pltpu.make_async_copy(source, target, small_sem.at[i])
        for i, (source, target) in enumerate(
            [
                (langs_hbm, langs_ref),
                (lens_hbm, lens_ref),
                (rows_hbm, rows_ref),
                (map_hbm, map_ref),
                (pos_hbm, pos_ref),
                (gain_hbm, gain_ref),
                (bias_hbm, bias_ref),
            ]
        )
    ]
    for copy in small[:3]:
        copy.start()

    small_mesh = (n_seq, n_lang, n_panel) == (4, 2, 2)
    order = [3, 2, 1, 0] if small_mesh else list(range(n_seq))
    splits = SPLITS if small_mesh else ()

    def jobs_of(j):
        if not small_mesh:
            return [(j, slice(0, width), False)]
        found, first, index = [], 0, sum(len(split) for split in splits[:j])
        for place_of, columns in enumerate(splits[j]):
            columns = columns * width // 1024
            if columns:
                at = slice(first, first + columns)
                found.append((index + place_of, at, place_of == 1))
            first += columns
        return found

    def flip(index, bits):
        other = index
        for bit in (1, 2):
            if bits & bit:
                other = other + bit - 2 * bit * lax.rem(index // bit, 2)
        return other

    def to_seq(step):
        return flip(s, step) if small_mesh else lax.rem(s + step, n_seq)

    def peer(step):
        if small_mesh:
            at = (flip(s, step // 2), flip(l, step % 2))
            return at[0] * n_lang + at[1], {"seq": at[0], "lang": at[1]}
        other = lax.rem(chip + step, chips)
        return other, {"seq": other // n_lang, "lang": lax.rem(other, n_lang)}

    def from_peer(step):
        return peer(step)[0] if small_mesh else lax.rem(chip + chips - step, chips)

    def for_peers(body, first=1, last=chips):
        if small_mesh:
            for step in reversed(range(first, last)):
                body(step)
        else:
            lax.fori_loop(first, last, lambda step, carry: (body(step), carry)[1], 0)

    def for_part(first, last, body):
        if small_mesh:
            for j in range(first, last):
                body(j, order[j])
        else:
            lax.fori_loop(
                first,
                last,
                lambda j, carry: (body(j, lax.rem(j + 1, n_seq)), carry)[1],
                0,
            )

    barrier = pltpu.get_barrier_semaphore()

    def greet(step):
        pl.semaphore_signal(barrier, inc=1, device_id=peer(step)[1], device_id_type=MESH)

    for_peers(greet)
    pl.semaphore_signal(
        barrier, inc=1, device_id={"panel": other_core}, device_id_type=MESH
    )
    for copy in small[3:]:
        copy.start()
    for k in range(taps):
        conv_copy(k).start()
    down_copy.start()
    for copy in small[:3]:
        copy.wait()

    row_i, lane_i = iota((rows, 128), 0), iota((rows, 128), 1)
    meta = jnp.zeros((rows, 128), F32)
    for r in range(rows):
        meta = jnp.where((row_i == r) & (lane_i == 0), langs_ref[r].astype(F32), meta)
        meta = jnp.where((row_i == r) & (lane_i == 1), lens_ref[r].astype(F32), meta)
    send_rows[:, :width] = rows_ref[...]
    send_rows[:, width:] = meta.astype(BF16)
    recv_rows[p, chip] = send_rows[...]
    pl.semaphore_wait(barrier, chips)

    def row_copy(step, source):
        return pltpu.make_async_remote_copy(
            src_ref=send_rows,
            dst_ref=recv_rows.at[p, source],
            send_sem=row_send.at[step],
            recv_sem=row_recv.at[source],
            device_id=peer(step)[1],
            device_id_type=MESH,
        )

    for_peers(lambda step: row_copy(step, chip).start())

    spans = PARTS if small_mesh else 1
    span = chips // spans

    def pass_copy(which):
        at = pl.ds((s // 2 if which == 0 else 1 - s // 2) * span if spans == 2 else 0, span)
        return pltpu.make_async_remote_copy(
            src_ref=recv_rows.at[p, at],
            dst_ref=recv_rows.at[p, at],
            send_sem=pass_send.at[which],
            recv_sem=pass_recv.at[which],
            device_id={"panel": other_core},
            device_id_type=MESH,
        )

    def pass_arrival(which):
        at = pl.ds((s // 2 if which == 0 else 1 - s // 2) * span if spans == 2 else 0, span)
        return pltpu.make_async_remote_copy(
            src_ref=recv_rows.at[other_core, at],
            dst_ref=recv_rows.at[other_core, at],
            send_sem=pass_send.at[which],
            recv_sem=pass_recv.at[which],
            device_id={"panel": other_core},
            device_id_type=MESH,
        )

    for copy in small[3:]:
        copy.wait()

    lens_col = meta[:, 1:2]
    r0, r1 = iota((rows, rows), 0), iota((rows, rows), 1)
    own_len = jnp.sum(jnp.where(r0 == r1, lens_col, 0.0), axis=0, keepdims=True)
    own_start = jnp.sum(jnp.where(r0 < r1, lens_col, 0.0), axis=0, keepdims=True)
    f_i = iota((FR_DEV, rows), 0).astype(F32)
    inside = (f_i >= own_start) & (f_i < own_start + own_len)
    inside_f = jnp.where(inside, 1.0, 0.0)
    t_col = jnp.sum(jnp.where(inside, f_i - own_start, 0.0), axis=1, keepdims=True)
    mine32 = rows_ref[...].astype(F32)
    total = jnp.zeros((FR_DEV, width), F32)
    for r in range(rows):
        total = jnp.where(inside_f[:, r : r + 1] > 0.5, mine32[r : r + 1, :], total)
    where_pos = jnp.zeros((FR_DEV, width), F32)
    for t in range(slots):
        where_pos = jnp.where(t_col == float(t), pos_ref[t : t + 1, :], where_pos)
    own[...] = total + where_pos

    zero = jnp.zeros((reach * held, width), BF16)
    for g in range(HALVES):
        frames[g, : reach * held, :] = zero
        frames[g, (reach + slots) * held :, :] = zero

    my_lang = jnp.int32(0)
    for i in range(n_slot):
        my_lang = my_lang + jnp.where(map_ref[i] == slot, i, 0)
    my_lang = my_lang.astype(F32)
    b0, b1 = iota((block, block), 0), iota((block, block), 1)
    same_device = b0 // rows == b1 // rows
    device_start = (iota((1, block), 1) // rows * FR_DEV).astype(F32)
    k_i = iota((cap, block), 0).astype(F32)
    g_i = iota((block_frames, block), 0).astype(F32)
    c_i = iota((block_frames, cap * slots), 1).astype(F32)

    def pick(j, step):
        q = to_seq(step)
        part = jnp.concatenate(
            [
                recv_rows[b, q * n_lang + a].astype(F32)
                for a in range(n_lang)
                for b in range(n_panel)
            ],
            axis=0,
        )
        lang_col, len_col = part[:, width : width + 1], part[:, width + 1 : width + 2]
        is_mine = jnp.where(lang_col == my_lang, 1.0, 0.0)
        mine_row = jnp.sum(jnp.where(b0 == b1, is_mine, 0.0), axis=0, keepdims=True)
        rank = jnp.sum(jnp.where(b0 < b1, is_mine, 0.0), axis=0, keepdims=True)
        len_row = jnp.sum(jnp.where(b0 == b1, len_col, 0.0), axis=0, keepdims=True)
        start = device_start + jnp.sum(
            jnp.where(same_device & (b0 < b1), len_col, 0.0), axis=0, keepdims=True
        )
        picked = (mine_row > 0.5) & (rank == k_i)
        picked_bf = jnp.where(picked, 1.0, 0.0).astype(BF16)
        at = pl.ds(pl.multiple_of(j * cap, cap), cap)
        chosen[at, :] = jnp.dot(
            picked_bf, part[:, :width].astype(BF16), preferred_element_type=F32
        )
        row_len = jnp.sum(jnp.where(picked, len_row, 0.0), axis=1, keepdims=True)
        chosen_len[at, :] = jnp.broadcast_to(row_len, (cap, 128))
        here = (g_i >= start) & (g_i < start + len_row) & (mine_row > 0.5)
        column = jnp.sum(
            jnp.where(here, (g_i - start) * cap + rank + 1.0, 0.0), axis=1, keepdims=True
        )
        place[j] = jnp.where(c_i + 1.0 == column, 1.0, 0.0).astype(BF16)


    gain = gain_ref[...]

    def normalize(g):
        base = chosen[g * held : (g + 1) * held, :]
        limit = chosen_len[g * held : (g + 1) * held, 0:1]
        for t in range(slots):
            values = base + pos_ref[t : t + 1, :]
            center = values - jnp.mean(values, axis=-1, keepdims=True)
            spread = jnp.mean(center * center, axis=-1, keepdims=True)
            normed = center * lax.rsqrt(spread + 1e-05) * gain
            normed = jnp.where(limit > float(t), normed, 0.0)
            frames[g, (reach + t) * held : (reach + t + 1) * held, :] = normed.astype(BF16)

    def convolve(g, first, last):
        if g == 0:
            for k in range(first, last):
                conv_copy(k).wait()
        for k in range(first, last):
            term = jnp.dot(
                frames[g, k * held : (k + slots) * held, :],
                conv[k],
                preferred_element_type=F32,
            )
            acc[g] = term + (bias_ref[...] if k == 0 else acc[g])

    def project(g):
        pre = acc[g]
        act = 0.5 * pre * (1.0 + lax.erf(pre * 0.7071067811865476))
        hidden[g] = act.astype(BF16)
        if g == 0:
            down_copy.wait()
        part32[g] = jnp.dot(hidden[g], down[...], preferred_element_type=F32)

    def core_copy(j, step):
        return pltpu.make_async_remote_copy(
            src_ref=packed.at[to_seq(step), other_core],
            dst_ref=from_core.at[j],
            send_sem=core_send.at[j],
            recv_sem=core_recv.at[j],
            device_id={"panel": other_core},
            device_id_type=MESH,
        )

    def lang_copy(j, step, job, turn):
        index, at, direct = job
        other = lax.rem(l + turn, n_lang)
        return pltpu.make_async_remote_copy(
            src_ref=packed.at[to_seq(step), p, other, :, at],
            dst_ref=from_lang.at[j, turn - 1, :, at],
            send_sem=lang_send.at[index, turn - 1],
            recv_sem=lang_recv.at[index, turn - 1],
            device_id={"lang": other, "seq": to_seq(step)} if direct else {"lang": other},
            device_id_type=MESH,
        )

    def seq_copy(j, step, job):
        index, at, _ = job
        other = to_seq(step)
        return pltpu.make_async_remote_copy(
            src_ref=packed.at[other, p, l, :, at],
            dst_ref=from_seq.at[j, :, at],
            send_sem=seq_send.at[index],
            recv_sem=seq_recv.at[index],
            device_id={"seq": other},
            device_id_type=MESH,
        )

    def pack(g, j, step):
        q = to_seq(step)
        pieces = [
            part32[g, pl.ds(pl.multiple_of(t * held + (j - g * half) * cap, cap), cap), :]
            for t in range(slots)
        ]
        mine = jnp.concatenate(pieces, axis=0).astype(BF16)
        moved = jnp.dot(place[j], mine, preferred_element_type=F32).astype(BF16)
        for a in range(n_lang):
            for b in range(n_panel):
                first = (a * n_panel + b) * FR_DEV
                packed[q, b, a] = moved[first : first + FR_DEV, :]
        core_copy(j, step).start()

    def after_core(j, step):
        core_copy(j, step).wait_recv()
        q = to_seq(step)
        packed[q, p] = packed[q, p] + from_core[j]
        for job in jobs_of(j):
            for turn in range(1, n_lang):
                lang_copy(j, step, job, turn).start()

    def straight(j, step):
        for job in jobs_of(j):
            if job[2]:
                seq_copy(j, step, job).start()

    def add_lang(j, step, job):
        at = job[1]
        total = packed[to_seq(step), p, l, :, at]
        for turn in range(1, n_lang):
            lang_copy(j, step, job, turn).wait_recv()
            total = total + from_lang[j, turn - 1, :, at]
        return total

    def after_lang(j, step):
        for job in jobs_of(j):
            if not job[2]:
                packed[to_seq(step), p, l, :, job[1]] = add_lang(j, step, job)
                seq_copy(j, step, job).start()

    def arrive(first, last):
        for_peers(lambda step: row_copy(step, from_peer(step)).wait_recv(), first, last)

    if spans == 2:
        arrive(1, span)
        pass_copy(0).start()
        arrive(span, chips)
        pass_copy(1).start()
        pass_arrival(0).wait_recv()
        for_part(half, n_seq, pick)
        normalize(1)
        pass_arrival(1).wait_recv()
        for_part(0, half, pick)
        normalize(0)
    else:
        arrive(1, chips)
        pass_copy(0).start()
        pass_arrival(0).wait_recv()
        for_part(0, n_seq, pick)
        normalize(0)
        normalize(1)
    convolve(0, 0, taps)
    project(0)
    for_part(0, half, functools.partial(pack, 0))
    convolve(1, 0, BREAK)
    for_part(0, half, after_core)
    for_part(0, half, straight)
    convolve(1, BREAK, taps)
    project(1)
    for_part(half, n_seq, functools.partial(pack, 1))
    for_part(half, n_seq, after_core)
    for_part(half, n_seq, straight)
    for_part(0, half, after_lang)
    for_part(half, n_seq - 1, after_lang)
    own_job = jobs_of(n_seq - 1)[0]
    own[...] += add_lang(n_seq - 1, 0, own_job).astype(F32)

    def after_seq(j, step):
        for job in jobs_of(j):
            at = job[1]
            seq_copy(j, step, job).wait_recv()
            total = own[:, at] + from_seq[j, :, at].astype(F32)
            if job[2]:
                for turn in range(1, n_lang):
                    lang_copy(j, step, job, turn).wait_recv()
                    total = total + from_lang[j, turn - 1, :, at].astype(F32)
            own[:, at] = total

    for_part(0, n_seq - 1, after_seq)
    out_ref[...] = own[...].astype(BF16)

    def sent(j, step):
        core_copy(j, step).wait_send()
        for job in jobs_of(j):
            for turn in range(1, n_lang):
                lang_copy(j, step, job, turn).wait_send()

    def seq_sent(j, step):
        for job in jobs_of(j):
            seq_copy(j, step, job).wait_send()

    for_peers(lambda step: row_copy(step, chip).wait_send())
    for which in range(spans):
        pass_copy(which).wait_send()
    for_part(0, n_seq, sent)
    for_part(0, n_seq - 1, seq_sent)


def per_device(
    sizes,
    text_rows,
    lang_ids,
    lang_map,
    durations,
    pos_table,
    ln_gain,
    conv_weight,
    conv_bias,
    down_weight,
):
    n_seq, n_lang, n_panel = sizes
    chips = n_seq * n_lang
    rows, width = text_rows.shape
    slots = pos_table.shape[0]
    taps, hidden_width = conv_weight.shape[2], conv_weight.shape[3]
    cap = 2 * rows
    held = cap * n_seq
    n_slot = n_lang * n_panel
    dma = pltpu.SemaphoreType.DMA
    vmem = pl.BlockSpec(memory_space=pltpu.VMEM)
    hbm = pl.BlockSpec(memory_space=pl.ANY)
    return pl.pallas_call(
        functools.partial(layer_kernel, sizes),
        out_shape=pltpu.VMEM((FR_DEV, width), BF16),
        in_specs=[hbm] * 9,
        out_specs=vmem,
        scratch_shapes=[
            pltpu.SMEM((rows,), jnp.int32),
            pltpu.SMEM(lang_map.shape, jnp.int32),
            pltpu.SMEM((rows,), jnp.int32),
            pltpu.VMEM((rows, width), BF16),
            pltpu.VMEM((slots, width), F32),
            pltpu.VMEM((1, width), F32),
            pltpu.VMEM((1, hidden_width), F32),
            dma((7,)),
            pltpu.VMEM((taps, width, hidden_width), BF16),
            pltpu.VMEM((hidden_width, width), BF16),
            pltpu.VMEM((rows, width + 128), BF16),
            pltpu.VMEM((n_panel, chips, rows, width + 128), BF16),
            pltpu.VMEM((held, width), F32),
            pltpu.VMEM((held, 128), F32),
            pltpu.VMEM((n_seq, FR_DEV * n_slot, cap * slots), BF16),
            pltpu.VMEM((HALVES, (slots + taps - 1) * held // HALVES, width), BF16),
            pltpu.VMEM((HALVES, held * slots // HALVES, hidden_width), F32),
            pltpu.VMEM((HALVES, held * slots // HALVES, hidden_width), BF16),
            pltpu.VMEM((HALVES, held * slots // HALVES, width), F32),
            pltpu.VMEM((FR_DEV, width), F32),
            pltpu.VMEM((n_seq, n_panel, n_lang, FR_DEV, width), BF16),
            pltpu.VMEM((n_seq, n_lang, FR_DEV, width), BF16),
            pltpu.VMEM((n_seq, n_lang - 1, FR_DEV, width), BF16),
            pltpu.VMEM((n_seq - 1, FR_DEV, width), BF16),
            dma((taps,)),
            dma(()),
            dma((chips,)),
            dma((chips,)),
            dma((PARTS,)),
            dma((PARTS,)),
            dma((n_seq,)),
            dma((n_seq,)),
            dma((n_seq + 4, n_lang - 1)),
            dma((n_seq + 4, n_lang - 1)),
            dma((n_seq + 4,)),
            dma((n_seq + 4,)),
        ],
        compiler_params=pltpu.CompilerParams(
            collective_id=0, has_side_effects=True, vmem_limit_bytes=58 * 1024 * 1024
        ),
    )(
        lang_ids.reshape(rows),
        lang_map,
        durations.reshape(rows),
        text_rows,
        pos_table,
        ln_gain.reshape(1, width),
        conv_bias,
        jnp.transpose(conv_weight[0], (1, 0, 2)),
        down_weight[0],
    )


def solution(mesh):
    sizes = (mesh.shape["seq"], mesh.shape["lang"], mesh.shape["panel"])
    return jax.shard_map(
        functools.partial(per_device, sizes),
        mesh=mesh,
        in_specs=(
            P(("groups", "seq", "lang", "panel"), None),
            P(("groups", "seq", "lang", "panel"), None),
            P(),
            P(("groups", "seq", "lang", "panel"), None),
            P(),
            P(),
            P(("lang", "panel"), None, None, "seq"),
            P(("lang", "panel"), "seq"),
            P(("lang", "panel"), "seq", None),
        ),
        out_specs=P(("groups", "seq", "lang", "panel"), None),
        check_vma=False,
    )
```

```python
import functools

import jax
import jax.numpy as jnp
from jax import lax
from jax.experimental import pallas as pl
from jax.experimental.pallas import tpu as pltpu
from jax.sharding import PartitionSpec as P

MESH = pl.DeviceIdType.MESH
FR_DEV = 24
HALVES = 2
BREAK = 4
PARTS = 2
SPLITS = ((0, 1024), (1024,), (0, 1024), (1024,))
F32 = jnp.float32
BF16 = jnp.bfloat16


def iota(shape, dim):
    return lax.broadcasted_iota(jnp.int32, shape, dim)


def layer_kernel(
    sizes,
    langs_hbm,
    map_hbm,
    lens_hbm,
    rows_hbm,
    pos_hbm,
    gain_hbm,
    bias_hbm,
    conv_hbm,
    down_hbm,
    out_ref,
    langs_ref,
    map_ref,
    lens_ref,
    rows_ref,
    pos_ref,
    gain_ref,
    bias_ref,
    small_sem,
    conv,
    down,
    send_rows,
    recv_rows,
    chosen,
    chosen_len,
    place,
    frames,
    acc,
    hidden,
    part32,
    own,
    packed,
    from_core,
    from_lang,
    from_seq,
    conv_sem,
    down_sem,
    row_send,
    row_recv,
    pass_send,
    pass_recv,
    core_send,
    core_recv,
    lang_send,
    lang_recv,
    seq_send,
    seq_recv,
):
    n_seq, n_lang, n_panel = sizes
    n_slot = n_lang * n_panel
    rows, width = rows_ref.shape
    slots = pos_ref.shape[0]
    taps = conv.shape[0]
    cap = 2 * rows
    half = n_seq // HALVES
    held = cap * half
    block = rows * n_slot
    block_frames = FR_DEV * n_slot
    reach = taps // 2
    s = lax.axis_index("seq")
    l = lax.axis_index("lang")
    p = lax.axis_index("panel")
    slot = l * n_panel + p
    chips = n_seq * n_lang
    chip = s * n_lang + l
    other_core = lax.rem(p + 1, n_panel)

    def conv_copy(k):
        return pltpu.make_async_copy(conv_hbm.at[k], conv.at[k], conv_sem.at[k])

    down_copy = pltpu.make_async_copy(down_hbm, down, down_sem)
    small = [
        pltpu.make_async_copy(source, target, small_sem.at[i])
        for i, (source, target) in enumerate(
            [
                (langs_hbm, langs_ref),
                (lens_hbm, lens_ref),
                (rows_hbm, rows_ref),
                (map_hbm, map_ref),
                (pos_hbm, pos_ref),
                (gain_hbm, gain_ref),
                (bias_hbm, bias_ref),
            ]
        )
    ]
    for copy in small[:3]:
        copy.start()

    small_mesh = (n_seq, n_lang, n_panel) == (4, 2, 2)
    order = [3, 2, 1, 0] if small_mesh else list(range(n_seq))
    splits = SPLITS if small_mesh else ()

    def jobs_of(j):
        if not small_mesh:
            return [(j, slice(0, width), False)]
        found, first, index = [], 0, sum(len(split) for split in splits[:j])
        for place_of, columns in enumerate(splits[j]):
            columns = columns * width // 1024
            if columns:
                at = slice(first, first + columns)
                found.append((index + place_of, at, place_of == 1))
            first += columns
        return found

    def flip(index, bits):
        other = index
        for bit in (1, 2):
            if bits & bit:
                other = other + bit - 2 * bit * lax.rem(index // bit, 2)
        return other

    def to_seq(step):
        return flip(s, step) if small_mesh else lax.rem(s + step, n_seq)

    def peer(step):
        if small_mesh:
            at = (flip(s, step // 2), flip(l, step % 2))
            return at[0] * n_lang + at[1], {"seq": at[0], "lang": at[1]}
        other = lax.rem(chip + step, chips)
        return other, {"seq": other // n_lang, "lang": lax.rem(other, n_lang)}

    def from_peer(step):
        return peer(step)[0] if small_mesh else lax.rem(chip + chips - step, chips)

    def for_peers(body, first=1, last=chips):
        if small_mesh:
            for step in reversed(range(first, last)):
                body(step)
        else:
            lax.fori_loop(first, last, lambda step, carry: (body(step), carry)[1], 0)

    def for_part(first, last, body):
        if small_mesh:
            for j in range(first, last):
                body(j, order[j])
        else:
            lax.fori_loop(
                first,
                last,
                lambda j, carry: (body(j, lax.rem(j + 1, n_seq)), carry)[1],
                0,
            )

    barrier = pltpu.get_barrier_semaphore()

    def greet(step):
        pl.semaphore_signal(barrier, inc=1, device_id=peer(step)[1], device_id_type=MESH)

    for_peers(greet)
    pl.semaphore_signal(
        barrier, inc=1, device_id={"panel": other_core}, device_id_type=MESH
    )
    for copy in small[3:]:
        copy.start()
    for k in range(taps):
        conv_copy(k).start()
    down_copy.start()
    for copy in small[:3]:
        copy.wait()

    row_i, lane_i = iota((rows, 128), 0), iota((rows, 128), 1)
    meta = jnp.zeros((rows, 128), F32)
    for r in range(rows):
        meta = jnp.where((row_i == r) & (lane_i == 0), langs_ref[r].astype(F32), meta)
        meta = jnp.where((row_i == r) & (lane_i == 1), lens_ref[r].astype(F32), meta)
    send_rows[:, :width] = rows_ref[...]
    send_rows[:, width:] = meta.astype(BF16)
    recv_rows[p, chip] = send_rows[...]
    pl.semaphore_wait(barrier, chips)

    def row_copy(step, source):
        return pltpu.make_async_remote_copy(
            src_ref=send_rows,
            dst_ref=recv_rows.at[p, source],
            send_sem=row_send.at[step],
            recv_sem=row_recv.at[source],
            device_id=peer(step)[1],
            device_id_type=MESH,
        )

    for_peers(lambda step: row_copy(step, chip).start())

    spans = PARTS if small_mesh else 1
    span = chips // spans

    def pass_copy(which):
        at = pl.ds((s // 2 if which == 0 else 1 - s // 2) * span if spans == 2 else 0, span)
        return pltpu.make_async_remote_copy(
            src_ref=recv_rows.at[p, at],
            dst_ref=recv_rows.at[p, at],
            send_sem=pass_send.at[which],
            recv_sem=pass_recv.at[which],
            device_id={"panel": other_core},
            device_id_type=MESH,
        )

    def pass_arrival(which):
        at = pl.ds((s // 2 if which == 0 else 1 - s // 2) * span if spans == 2 else 0, span)
        return pltpu.make_async_remote_copy(
            src_ref=recv_rows.at[other_core, at],
            dst_ref=recv_rows.at[other_core, at],
            send_sem=pass_send.at[which],
            recv_sem=pass_recv.at[which],
            device_id={"panel": other_core},
            device_id_type=MESH,
        )

    for copy in small[3:]:
        copy.wait()

    lens_col = meta[:, 1:2]
    r0, r1 = iota((rows, rows), 0), iota((rows, rows), 1)
    own_len = jnp.sum(jnp.where(r0 == r1, lens_col, 0.0), axis=0, keepdims=True)
    own_start = jnp.sum(jnp.where(r0 < r1, lens_col, 0.0), axis=0, keepdims=True)
    f_i = iota((FR_DEV, rows), 0).astype(F32)
    inside = (f_i >= own_start) & (f_i < own_start + own_len)
    inside_f = jnp.where(inside, 1.0, 0.0)
    t_col = jnp.sum(jnp.where(inside, f_i - own_start, 0.0), axis=1, keepdims=True)
    mine32 = rows_ref[...].astype(F32)
    total = jnp.zeros((FR_DEV, width), F32)
    for r in range(rows):
        total = jnp.where(inside_f[:, r : r + 1] > 0.5, mine32[r : r + 1, :], total)
    where_pos = jnp.zeros((FR_DEV, width), F32)
    for t in range(slots):
        where_pos = jnp.where(t_col == float(t), pos_ref[t : t + 1, :], where_pos)
    own[...] = total + where_pos

    zero = jnp.zeros((reach * held, width), BF16)
    for g in range(HALVES):
        frames[g, : reach * held, :] = zero
        frames[g, (reach + slots) * held :, :] = zero

    my_lang = jnp.int32(0)
    for i in range(n_slot):
        my_lang = my_lang + jnp.where(map_ref[i] == slot, i, 0)
    my_lang = my_lang.astype(F32)
    b0, b1 = iota((block, block), 0), iota((block, block), 1)
    same_device = b0 // rows == b1 // rows
    device_start = (iota((1, block), 1) // rows * FR_DEV).astype(F32)
    k_i = iota((cap, block), 0).astype(F32)
    g_i = iota((block_frames, block), 0).astype(F32)
    c_i = iota((block_frames, cap * slots), 1).astype(F32)

    def pick(j, step):
        q = to_seq(step)
        part = jnp.concatenate(
            [
                recv_rows[b, q * n_lang + a].astype(F32)
                for a in range(n_lang)
                for b in range(n_panel)
            ],
            axis=0,
        )
        lang_col, len_col = part[:, width : width + 1], part[:, width + 1 : width + 2]
        is_mine = jnp.where(lang_col == my_lang, 1.0, 0.0)
        mine_row = jnp.sum(jnp.where(b0 == b1, is_mine, 0.0), axis=0, keepdims=True)
        rank = jnp.sum(jnp.where(b0 < b1, is_mine, 0.0), axis=0, keepdims=True)
        len_row = jnp.sum(jnp.where(b0 == b1, len_col, 0.0), axis=0, keepdims=True)
        start = device_start + jnp.sum(
            jnp.where(same_device & (b0 < b1), len_col, 0.0), axis=0, keepdims=True
        )
        picked = (mine_row > 0.5) & (rank == k_i)
        picked_bf = jnp.where(picked, 1.0, 0.0).astype(BF16)
        at = pl.ds(pl.multiple_of(j * cap, cap), cap)
        chosen[at, :] = jnp.dot(
            picked_bf, part[:, :width].astype(BF16), preferred_element_type=F32
        )
        row_len = jnp.sum(jnp.where(picked, len_row, 0.0), axis=1, keepdims=True)
        chosen_len[at, :] = jnp.broadcast_to(row_len, (cap, 128))
        here = (g_i >= start) & (g_i < start + len_row) & (mine_row > 0.5)
        column = jnp.sum(
            jnp.where(here, (g_i - start) * cap + rank + 1.0, 0.0), axis=1, keepdims=True
        )
        place[j] = jnp.where(c_i + 1.0 == column, 1.0, 0.0).astype(BF16)


    gain = gain_ref[...]

    def normalize(g):
        base = chosen[g * held : (g + 1) * held, :]
        limit = chosen_len[g * held : (g + 1) * held, 0:1]
        for t in range(slots):
            values = base + pos_ref[t : t + 1, :]
            center = values - jnp.mean(values, axis=-1, keepdims=True)
            spread = jnp.mean(center * center, axis=-1, keepdims=True)
            normed = center * lax.rsqrt(spread + 1e-05) * gain
            normed = jnp.where(limit > float(t), normed, 0.0)
            frames[g, (reach + t) * held : (reach + t + 1) * held, :] = normed.astype(BF16)

    def convolve(g, first, last):
        if g == 0:
            for k in range(first, last):
                conv_copy(k).wait()
        for k in range(first, last):
            term = jnp.dot(
                frames[g, k * held : (k + slots) * held, :],
                conv[k],
                preferred_element_type=F32,
            )
            acc[g] = term + (bias_ref[...] if k == 0 else acc[g])

    def project(g):
        pre = acc[g]
        act = 0.5 * pre * (1.0 + lax.erf(pre * 0.7071067811865476))
        hidden[g] = act.astype(BF16)
        if g == 0:
            down_copy.wait()
        part32[g] = jnp.dot(hidden[g], down[...], preferred_element_type=F32)

    def core_copy(j, step):
        return pltpu.make_async_remote_copy(
            src_ref=packed.at[to_seq(step), other_core],
            dst_ref=from_core.at[j],
            send_sem=core_send.at[j],
            recv_sem=core_recv.at[j],
            device_id={"panel": other_core},
            device_id_type=MESH,
        )

    def lang_copy(j, step, job, turn):
        index, at, direct = job
        other = lax.rem(l + turn, n_lang)
        return pltpu.make_async_remote_copy(
            src_ref=packed.at[to_seq(step), p, other, :, at],
            dst_ref=from_lang.at[j, turn - 1, :, at],
            send_sem=lang_send.at[index, turn - 1],
            recv_sem=lang_recv.at[index, turn - 1],
            device_id={"lang": other, "seq": to_seq(step)} if direct else {"lang": other},
            device_id_type=MESH,
        )

    def seq_copy(j, step, job):
        index, at, _ = job
        other = to_seq(step)
        return pltpu.make_async_remote_copy(
            src_ref=packed.at[other, p, l, :, at],
            dst_ref=from_seq.at[j, :, at],
            send_sem=seq_send.at[index],
            recv_sem=seq_recv.at[index],
            device_id={"seq": other},
            device_id_type=MESH,
        )

    def pack(g, j, step):
        q = to_seq(step)
        pieces = [
            part32[g, pl.ds(pl.multiple_of(t * held + (j - g * half) * cap, cap), cap), :]
            for t in range(slots)
        ]
        mine = jnp.concatenate(pieces, axis=0).astype(BF16)
        moved = jnp.dot(place[j], mine, preferred_element_type=F32).astype(BF16)
        for a in range(n_lang):
            for b in range(n_panel):
                first = (a * n_panel + b) * FR_DEV
                packed[q, b, a] = moved[first : first + FR_DEV, :]
        core_copy(j, step).start()

    def after_core(j, step):
        core_copy(j, step).wait_recv()
        q = to_seq(step)
        packed[q, p] = packed[q, p] + from_core[j]
        for job in jobs_of(j):
            for turn in range(1, n_lang):
                lang_copy(j, step, job, turn).start()

    def straight(j, step):
        for job in jobs_of(j):
            if job[2]:
                seq_copy(j, step, job).start()

    def add_lang(j, step, job):
        at = job[1]
        total = packed[to_seq(step), p, l, :, at]
        for turn in range(1, n_lang):
            lang_copy(j, step, job, turn).wait_recv()
            total = total + from_lang[j, turn - 1, :, at]
        return total

    def after_lang(j, step):
        for job in jobs_of(j):
            if not job[2]:
                packed[to_seq(step), p, l, :, job[1]] = add_lang(j, step, job)
                seq_copy(j, step, job).start()

    def arrive(first, last):
        for_peers(lambda step: row_copy(step, from_peer(step)).wait_recv(), first, last)

    if spans == 2:
        arrive(1, span)
        pass_copy(0).start()
        arrive(span, chips)
        pass_copy(1).start()
        pass_arrival(0).wait_recv()
        for_part(half, n_seq, pick)
        normalize(1)
        pass_arrival(1).wait_recv()
        for_part(0, half, pick)
        normalize(0)
    else:
        arrive(1, chips)
        pass_copy(0).start()
        pass_arrival(0).wait_recv()
        for_part(0, n_seq, pick)
        normalize(0)
        normalize(1)
    convolve(0, 0, taps)
    project(0)
    for_part(0, half, functools.partial(pack, 0))
    convolve(1, 0, BREAK)
    for_part(0, half, after_core)
    for_part(0, half, straight)
    convolve(1, BREAK, taps)
    project(1)
    for_part(half, n_seq, functools.partial(pack, 1))
    for_part(half, n_seq, after_core)
    for_part(half, n_seq, straight)
    for_part(0, half, after_lang)
    for_part(half, n_seq - 1, after_lang)
    own_job = jobs_of(n_seq - 1)[0]
    own[...] += add_lang(n_seq - 1, 0, own_job).astype(F32)

    def after_seq(j, step):
        for job in jobs_of(j):
            at = job[1]
            seq_copy(j, step, job).wait_recv()
            total = own[:, at] + from_seq[j, :, at].astype(F32)
            if job[2]:
                for turn in range(1, n_lang):
                    lang_copy(j, step, job, turn).wait_recv()
                    total = total + from_lang[j, turn - 1, :, at].astype(F32)
            own[:, at] = total

    def sent(j, step):
        core_copy(j, step).wait_send()
        for job in jobs_of(j):
            for turn in range(1, n_lang):
                lang_copy(j, step, job, turn).wait_send()

    for_peers(lambda step: row_copy(step, chip).wait_send())
    for which in range(spans):
        pass_copy(which).wait_send()
    for_part(0, n_seq, sent)
    if small_mesh:
        for_part(half, n_seq - 1, after_seq)
        for_part(0, half, after_seq)
    else:
        for_part(0, n_seq - 1, after_seq)
    out_ref[...] = own[...].astype(BF16)

    def seq_sent(j, step):
        for job in jobs_of(j):
            seq_copy(j, step, job).wait_send()

    for_part(0, n_seq - 1, seq_sent)


def per_device(
    sizes,
    text_rows,
    lang_ids,
    lang_map,
    durations,
    pos_table,
    ln_gain,
    conv_weight,
    conv_bias,
    down_weight,
):
    n_seq, n_lang, n_panel = sizes
    chips = n_seq * n_lang
    rows, width = text_rows.shape
    slots = pos_table.shape[0]
    taps, hidden_width = conv_weight.shape[2], conv_weight.shape[3]
    cap = 2 * rows
    held = cap * n_seq
    n_slot = n_lang * n_panel
    dma = pltpu.SemaphoreType.DMA
    vmem = pl.BlockSpec(memory_space=pltpu.VMEM)
    hbm = pl.BlockSpec(memory_space=pl.ANY)
    return pl.pallas_call(
        functools.partial(layer_kernel, sizes),
        out_shape=pltpu.VMEM((FR_DEV, width), BF16),
        in_specs=[hbm] * 9,
        out_specs=vmem,
        scratch_shapes=[
            pltpu.SMEM((rows,), jnp.int32),
            pltpu.SMEM(lang_map.shape, jnp.int32),
            pltpu.SMEM((rows,), jnp.int32),
            pltpu.VMEM((rows, width), BF16),
            pltpu.VMEM((slots, width), F32),
            pltpu.VMEM((1, width), F32),
            pltpu.VMEM((1, hidden_width), F32),
            dma((7,)),
            pltpu.VMEM((taps, width, hidden_width), BF16),
            pltpu.VMEM((hidden_width, width), BF16),
            pltpu.VMEM((rows, width + 128), BF16),
            pltpu.VMEM((n_panel, chips, rows, width + 128), BF16),
            pltpu.VMEM((held, width), F32),
            pltpu.VMEM((held, 128), F32),
            pltpu.VMEM((n_seq, FR_DEV * n_slot, cap * slots), BF16),
            pltpu.VMEM((HALVES, (slots + taps - 1) * held // HALVES, width), BF16),
            pltpu.VMEM((HALVES, held * slots // HALVES, hidden_width), F32),
            pltpu.VMEM((HALVES, held * slots // HALVES, hidden_width), BF16),
            pltpu.VMEM((HALVES, held * slots // HALVES, width), F32),
            pltpu.VMEM((FR_DEV, width), F32),
            pltpu.VMEM((n_seq, n_panel, n_lang, FR_DEV, width), BF16),
            pltpu.VMEM((n_seq, n_lang, FR_DEV, width), BF16),
            pltpu.VMEM((n_seq, n_lang - 1, FR_DEV, width), BF16),
            pltpu.VMEM((n_seq - 1, FR_DEV, width), BF16),
            dma((taps,)),
            dma(()),
            dma((chips,)),
            dma((chips,)),
            dma((PARTS,)),
            dma((PARTS,)),
            dma((n_seq,)),
            dma((n_seq,)),
            dma((n_seq + 4, n_lang - 1)),
            dma((n_seq + 4, n_lang - 1)),
            dma((n_seq + 4,)),
            dma((n_seq + 4,)),
        ],
        compiler_params=pltpu.CompilerParams(
            collective_id=0, has_side_effects=True, vmem_limit_bytes=58 * 1024 * 1024
        ),
    )(
        lang_ids.reshape(rows),
        lang_map,
        durations.reshape(rows),
        text_rows,
        pos_table,
        ln_gain.reshape(1, width),
        conv_bias,
        jnp.transpose(conv_weight[0], (1, 0, 2)),
        down_weight[0],
    )


def solution(mesh):
    sizes = (mesh.shape["seq"], mesh.shape["lang"], mesh.shape["panel"])
    return jax.shard_map(
        functools.partial(per_device, sizes),
        mesh=mesh,
        in_specs=(
            P(("groups", "seq", "lang", "panel"), None),
            P(("groups", "seq", "lang", "panel"), None),
            P(),
            P(("groups", "seq", "lang", "panel"), None),
            P(),
            P(),
            P(("lang", "panel"), None, None, "seq"),
            P(("lang", "panel"), "seq"),
            P(("lang", "panel"), "seq", None),
        ),
        out_specs=P(("groups", "seq", "lang", "panel"), None),
        check_vma=False,
    )
```
